128 devices in a mesh: seq: 32 (over y, x, core), hid: 4 (over z).
Axes of the slice: x: 4, y: 4, z: 4, core: 2. Of those that a mesh axis runs over, the one named last changes fastest.
Arguments:
- patches: bfloat16 [12288, 3200], P('seq'), may hold values from -6 to 6
- norm_gain: float32 [3200], replicated, may hold values from 0.5 to 8
- query_weight: bfloat16 [3200, 2048], P(None, 'hid'), may hold values from -0.109375 to 0.109375
- key_weight: bfloat16 [3200, 2048], P(None, 'hid'), may hold values from -0.7424621 to 0.7424621
- value_weight: bfloat16 [3200, 2048], P(None, 'hid'), may hold values from -0.109375 to 0.109375
- out_weight: bfloat16 [2048, 3200], P('hid'), may hold values from -0.125 to 0.125
- layer_scale: float32 [3200], replicated, may hold values from 0.3 to 1.5
- merge_gain: float32 [12800], P('hid'), may hold values from 0.5 to 1.5
- merge_bias: float32 [12800], P('hid'), may hold values from -3 to 3
- proj_weight: bfloat16 [12800, 6144], P('hid', 'seq'), may hold values from -0.0546875 to 0.0546875
- proj_bias: float32 [6144], P('seq'), may hold values from -3 to 3
- text_rows: bfloat16 [512, 6144], P(None, 'seq'), may hold values from -6 to 6
- stream_gain: float32 [6144], P('hid'), may hold values from 0.5 to 1.5
- tile_counts: int32 [3], replicated, may hold values from 1 to 7, as said below
- image_slots: int32 [3072], replicated, may hold values from 0 to 3583, as said below
- text_slots: int32 [512], replicated, may hold values from 0 to 3583, as said below
Outputs:
- stream: bfloat16 [3584, 6144], P('seq', 'hid')
- normed: bfloat16 [3584, 6144], P('seq', 'hid')
The draws below stay inside these ranges and needn't reach their ends.
Inputs may be any that keep to these rules, and one draw needn't show every extreme that they name: `tile_counts`: the tile counts sum to 12; the largest is exactly 7. `image_slots`: image slots and text slots together name every stream position once; each image's rows lie in order at consecutive positions. `text_slots`: see image_slots; text slots increase.
All inputs are finite; a program needn't handle non-finite values.
Results may differ from the reference program's by a relative error of at most 0.022.
The reference program's roundings to bfloat16 on the way (of `normed_in`, `attended`, `merged_normed` and `image_rows`) count: a program that leaves them out, or rounds other values in their place, can miss the bound.
Values may be sent and summed in bfloat16 or wider, within the bound.
No kernel may reach another device: no remote copies, remote signals or barrier semaphores. Data moves between devices by JAX's collectives and lax.ppermute only.
A program may use at most 192 MiB of HBM per device.

```python
import math
import jax
import jax.numpy as jnp
from jax import lax

D = 3200
HEADS = 16
HD = 128
OUT = 6144
SIDE = 32
PATCHES = 12288
TILES = 12
IMAGES = 3
MAXT = 7
IMAGE_TOKENS = 3072
MERGED = 12800
TEXT = 512
STREAM = 3584


def layout(key):
    base_key = jax.random.fold_in(key, 7)
    order_key, cut_key, split_key = jax.random.split(base_key, 3)
    ranks = jax.random.permutation(order_key, IMAGES).astype(jnp.int32)
    extra_total = TILES - MAXT - (IMAGES - 1)
    inner_cuts = jnp.sort(jax.random.randint(split_key, (IMAGES - 2,), 0, extra_total + 1).astype(jnp.int32))
    edges = jnp.concatenate([jnp.zeros((1,), jnp.int32), inner_cuts, jnp.full((1,), extra_total, jnp.int32)])
    shares = (edges[1:] - edges[:-1]).astype(jnp.int32)
    others = shares[jnp.clip(ranks - 1, 0, IMAGES - 2)]
    counts = jnp.where(ranks == 0, MAXT, 1 + others).astype(jnp.int32)
    cuts = jnp.sort(jax.random.randint(cut_key, (IMAGES,), 0, TEXT + 1).astype(jnp.int32))
    return (counts, cuts)


def draw_tile_counts(key, part):
    counts, cuts = layout(key)
    return counts


def draw_image_slots(key, part):
    counts, cuts = layout(key)
    bounds = jnp.cumsum(counts) * (SIDE * SIDE // 4)
    token_index = jnp.arange(IMAGE_TOKENS, dtype=jnp.int32)
    owner = jnp.sum((token_index[:, None] >= bounds[None, :]).astype(jnp.int32), axis=1)
    return (token_index + cuts[owner]).astype(jnp.int32)


def draw_text_slots(key, part):
    counts, cuts = layout(key)
    starts = jnp.concatenate([jnp.zeros((1,), jnp.int32), jnp.cumsum(counts) * (SIDE * SIDE // 4)]).astype(jnp.int32)
    text_index = jnp.arange(TEXT, dtype=jnp.int32)
    segment = jnp.sum((text_index[:, None] >= cuts[None, :]).astype(jnp.int32), axis=1)
    return (text_index + starts[segment]).astype(jnp.int32)


def draw_norm_gain(key, part):
    return jax.random.uniform(key, (D,), jnp.float32, 0.7, 1.3)


def draw_key_weight(key, part):
    shift_key, entry_key = jax.random.split(jax.random.fold_in(key, 11))
    strengths = jnp.array([1.0, 2.5, 4.5, 7.0], jnp.float32)
    offset = jax.random.randint(shift_key, (), 0, 4).astype(jnp.int32)
    head_index = jnp.arange(HEADS, dtype=jnp.int32)
    factor = jnp.repeat(strengths[(head_index + offset) % 4], HD)
    entries = jnp.clip(jax.random.normal(entry_key, (D, HEADS * HD), jnp.float32), -6.0, 6.0)
    return (entries * D ** (-0.5) * factor[None, :]).astype(jnp.bfloat16)


def level_of(rng, dims, cuts, least, largest):
    def one(dim, blocks):
        steps = jax.random.uniform(jax.random.fold_in(jax.random.fold_in(rng, 6), dim), (blocks,), jnp.float32, least / len(cuts), largest / len(cuts))
        return jnp.repeat(jnp.exp(steps), dims[dim] // blocks).reshape((-1,) + (1,) * (len(dims) - dim - 1))

    factor_of = one(*cuts[0])
    for cut in cuts[1:]:
        factor_of = factor_of * one(*cut)
    return factor_of


def centred(own_key, shape, scale, reach, cuts=(), kind=jnp.bfloat16):
    gain = level_of(own_key, shape, cuts, -0.22, 0.18) if cuts else 1.0
    values = jax.random.normal(own_key, shape, jnp.float32) * scale * gain
    return jnp.minimum(jnp.maximum(values, -reach), reach).astype(kind)


def setup_inputs(seed: int = 0) -> dict:
    arg_keys = jax.random.split(jax.random.key(seed), 17)
    return {
        "patches": centred(arg_keys[0], (PATCHES, D), 1.0, 6.0, ((0, 32),)),
        "norm_gain": draw_norm_gain(jax.random.fold_in(arg_keys[16], 71), 0),
        "query_weight": centred(arg_keys[2], (D, HEADS * HD), D ** -0.5, 0.109375, ((1, 4),)),
        "key_weight": draw_key_weight(jax.random.fold_in(arg_keys[16], 71), 0),
        "value_weight": centred(arg_keys[4], (D, HEADS * HD), D ** -0.5, 0.109375, ((1, 4),)),
        "out_weight": centred(arg_keys[5], (HEADS * HD, D), (HEADS * HD) ** -0.5, 0.125, ((0, 4),)),
        "layer_scale": jnp.clip(jnp.exp(jax.random.uniform(arg_keys[6], (D,), jnp.float32, math.log(0.3), math.log(1.5))), 0.3, 1.5),
        "merge_gain": jnp.clip(1.0 + 0.1 * jax.random.normal(arg_keys[7], (MERGED,), jnp.float32), 0.5, 1.5),
        "merge_bias": centred(arg_keys[8], (MERGED,), 0.5, 3.0, ((0, 4),), jnp.float32),
        "proj_weight": centred(arg_keys[9], (MERGED, OUT), MERGED ** -0.5, 0.0546875, ((0, 4), (1, 32))),
        "proj_bias": centred(arg_keys[10], (OUT,), 0.5, 3.0, ((0, 32),), jnp.float32),
        "text_rows": centred(arg_keys[11], (TEXT, OUT), 1.0, 6.0, ((1, 32),)),
        "stream_gain": jnp.clip(1.0 + 0.1 * jax.random.normal(arg_keys[12], (OUT,), jnp.float32), 0.5, 1.5),
        "tile_counts": draw_tile_counts(jax.random.fold_in(arg_keys[16], 71), 0),
        "image_slots": draw_image_slots(jax.random.fold_in(arg_keys[16], 71), 0),
        "text_slots": draw_text_slots(jax.random.fold_in(arg_keys[16], 71), 0),
    }


def image_of(index_rows, tile_counts):
    bounds = jnp.cumsum(tile_counts) * (SIDE * SIDE)
    return lax.optimization_barrier(jnp.sum((index_rows[:, None] >= bounds[None, :]).astype(jnp.int32), axis=1))

def shuffle_rows(values):
    row_count, width = values.shape
    grouped = values.reshape(row_count // (2 * SIDE), 2, SIDE // 2, 2, width)
    return grouped.transpose(0, 2, 4, 1, 3).reshape(row_count // 4, 4 * width)

def reference(patches, norm_gain, query_weight, key_weight, value_weight, out_weight, layer_scale, merge_gain, merge_bias, proj_weight, proj_bias, text_rows, stream_gain, tile_counts, image_slots, text_slots):
    tokens_f = patches.astype(jnp.float32)
    normed_in = (tokens_f * lax.rsqrt(lax.optimization_barrier(jnp.mean(tokens_f * tokens_f, -1, keepdims=True)) + 1e-06) * norm_gain).astype(jnp.bfloat16)
    queries = (jnp.dot(normed_in, query_weight, preferred_element_type=jnp.float32) * HD ** (-0.5)).astype(jnp.bfloat16)
    key_rows = jnp.dot(normed_in, key_weight, preferred_element_type=jnp.float32).astype(jnp.bfloat16)
    value_rows = jnp.dot(normed_in, value_weight, preferred_element_type=jnp.float32).astype(jnp.bfloat16)
    image_ids = image_of(jnp.arange(PATCHES, dtype=jnp.int32), tile_counts)
    same_image = image_ids[:, None] == image_ids[None, :]
    query_heads = queries.reshape(PATCHES, HEADS, HD).transpose(1, 0, 2)
    key_heads = key_rows.reshape(PATCHES, HEADS, HD).transpose(1, 0, 2)
    value_heads = value_rows.reshape(PATCHES, HEADS, HD).transpose(1, 0, 2)

    def one_head(operands):
        query_one, key_one, value_one = operands
        scores = jnp.dot(query_one, key_one.T, preferred_element_type=jnp.float32)
        scores = jnp.where(same_image, scores, jnp.float32(-1e+30))
        row_max = lax.optimization_barrier(jnp.max(scores, axis=1, keepdims=True))
        weights = jnp.where(same_image, jnp.exp(scores - row_max), jnp.float32(0.0))
        totals = lax.optimization_barrier(jnp.sum(weights, axis=1, keepdims=True))
        summed = jnp.dot(weights.astype(jnp.bfloat16), value_one, preferred_element_type=jnp.float32)
        return (summed / totals).astype(jnp.bfloat16)
    attended = lax.map(one_head, (query_heads, key_heads, value_heads))
    attended = attended.transpose(1, 0, 2).reshape(PATCHES, HEADS * HD)
    branch = jnp.dot(attended, out_weight, preferred_element_type=jnp.float32)
    residual = tokens_f + layer_scale * branch
    merged = shuffle_rows(residual)
    mean_row = lax.optimization_barrier(jnp.mean(merged, -1, keepdims=True))
    var_row = lax.optimization_barrier(jnp.mean(merged * merged, -1, keepdims=True)) - mean_row * mean_row
    merged_normed = ((merged - mean_row) * lax.rsqrt(var_row + 1e-05) * merge_gain + merge_bias).astype(jnp.bfloat16)
    projected = jnp.dot(merged_normed, proj_weight, preferred_element_type=jnp.float32) + proj_bias
    image_rows = jax.nn.gelu(projected, approximate=False).astype(jnp.bfloat16)
    stream = jnp.zeros((STREAM, OUT), jnp.bfloat16).at[image_slots].set(image_rows).at[text_slots].set(text_rows)
    stream_f = stream.astype(jnp.float32)
    normed = (stream_f * lax.rsqrt(lax.optimization_barrier(jnp.mean(stream_f * stream_f, -1, keepdims=True)) + 1e-05) * stream_gain).astype(jnp.bfloat16)
    return (stream, normed)
```

```python
import jax
import jax.numpy as jnp
from jax import lax
from jax.experimental import pallas as pl
from jax.experimental.pallas import tpu as pltpu
from jax.sharding import Mesh, PartitionSpec as P

HD = 128
ROWS = 384
MROWS = 96
BF = jnp.bfloat16
F32 = jnp.float32
LIMIT = 60 * 1024 * 1024


def cdot(a, b):
    return jnp.dot(a, b, preferred_element_type=F32)


def shift(value, axis, k):
    return lax.ppermute(value, axis, [(i, (i + k) % 4) for i in range(4)])


def swap(value):
    return lax.ppermute(value, "c", [(0, 1), (1, 0)])


def call(body, out_shape, scratch=(), **kw):
    return pl.pallas_call(
        body,
        out_shape=out_shape,
        scratch_shapes=scratch,
        compiler_params=pltpu.CompilerParams(vmem_limit_bytes=LIMIT),
        **kw,
    )


SMEM = pl.BlockSpec(memory_space=pltpu.SMEM)
VMEM = pl.BlockSpec(memory_space=pltpu.VMEM)
ANY = pl.BlockSpec(memory_space=pl.ANY)


def sub_row_permutation():
    row = lax.broadcasted_iota(jnp.int32, (ROWS, ROWS), 0)
    col = lax.broadcasted_iota(jnp.int32, (ROWS, ROWS), 1)
    sub = (row >= 96).astype(jnp.int32) + (row >= 192).astype(jnp.int32) + (row >= 288).astype(jnp.int32)
    m = row - 96 * sub
    source = (2 * (m >> 4) + (sub >> 1)) * 32 + 2 * (m & 15) + (sub & 1)
    return jnp.where(source == col, 1.0, 0.0).astype(BF)


def qkv_body(s_ref, x_ref, g_ref, wk_ref, wv_ref, wq_ref, kv_ref, q_ref, xn_ref):
    half = pl.program_id(0)

    @pl.when(half == 0)
    def _():
        xf = cdot(sub_row_permutation(), x_ref[...])
        scale = lax.rsqrt(jnp.mean(xf * xf, axis=-1, keepdims=True) + 1e-06)
        xn_ref[...] = (xf * scale * g_ref[...]).astype(BF)

    xn = xn_ref[...]
    keys = cdot(xn, wk_ref[...]).astype(BF)
    values = cdot(xn, wv_ref[...]).astype(BF)
    queries = (cdot(xn, wq_ref[...]) * HD ** (-0.5)).astype(BF)
    for i in range(2):
        slot = (2 * half + i - s_ref[0]) & 3
        part = slice(HD * i, HD * (i + 1))
        kv_ref[slot, :, 0:HD] = keys[:, part]
        kv_ref[slot, :, HD : 2 * HD] = values[:, part]
        q_ref[slot] = queries[:, part]


def project_qkv(y, patches, gain, wk, wv, wq):
    width = patches.shape[1]
    whole = pl.BlockSpec((ROWS, width), lambda j, s: (0, 0))
    weight = pl.BlockSpec((width, 2 * HD), lambda j, s: (0, j))
    return pl.pallas_call(
        qkv_body,
        out_shape=(
            jax.ShapeDtypeStruct((4, ROWS, 2 * HD), BF),
            jax.ShapeDtypeStruct((4, ROWS, HD), BF),
        ),
        grid_spec=pltpu.PrefetchScalarGridSpec(
            num_scalar_prefetch=1,
            grid=(2,),
            in_specs=[whole, pl.BlockSpec((1, width), lambda j, s: (0, 0)), weight, weight, weight],
            out_specs=[
                pl.BlockSpec((4, ROWS, 2 * HD), lambda j, s: (0, 0, 0)),
                pl.BlockSpec((4, ROWS, HD), lambda j, s: (0, 0, 0)),
            ],
            scratch_shapes=[pltpu.VMEM((ROWS, width), BF)],
        ),
        compiler_params=pltpu.CompilerParams(
            dimension_semantics=("arbitrary",), vmem_limit_bytes=LIMIT
        ),
    )(y, patches, gain, wk, wv, wq)


def attention_body(first, last, s_ref, q_ref, kvo_ref, kvs_ref, *refs):
    if first:
        rest = refs
    else:
        acc_in, max_in = refs[:2]
        rest = refs[2:]
    if last:
        o_ref, acc_ref, max_ref = rest
    else:
        acc_ref, max_ref = rest
    if first:
        acc_ref[...] = jnp.zeros(acc_ref.shape, F32)
        max_ref[...] = jnp.full(max_ref.shape, -1e30, F32)
    else:
        acc_ref[...] = acc_in[...]
        max_ref[...] = max_in[...]
    y, x, c, xk, bound0, bound1 = [s_ref[i] for i in range(6)]

    def image_of(row):
        return (row >= bound0).astype(jnp.int32) + (row >= bound1).astype(jnp.int32)

    def block(yy, xx, cc):
        base = ROWS * (8 * yy + 2 * xx + cc)
        return image_of(base), image_of(base + ROWS - 1), 1024 - (base & 1023)

    def row_images(info, dim):
        shape = (ROWS, 1) if dim == 0 else (1, ROWS)
        row = lax.broadcasted_iota(jnp.int32, shape, dim)
        sub = (row >= 96).astype(jnp.int32) + (row >= 192).astype(jnp.int32) + (row >= 288).astype(jnp.int32)
        m = row - 96 * sub
        return jnp.where(m * 4 < info[2], info[0], info[1])

    def update(qb, kb, masks):
        q = q_ref[qb]
        scores, values = [], []
        for n, ref in enumerate((kvo_ref, kvs_ref)):
            s = lax.dot_general(
                q, ref[kb, :, 0:HD], (((1,), (1,)), ((), ())), preferred_element_type=F32
            )
            if masks is not None:
                s = jnp.where(masks[n], s, -1e30)
            scores.append(s)
            values.append(
                jnp.concatenate([ref[kb, :, HD : 2 * HD], jnp.ones((ROWS, HD), BF)], axis=1)
            )
        old = max_ref[qb]
        top = jnp.maximum(
            jnp.max(scores[0], axis=1, keepdims=True), jnp.max(scores[1], axis=1, keepdims=True)
        )
        new = jnp.maximum(old, top)
        factor = jnp.exp(old - new)
        level = new[:, 0:1]
        acc = acc_ref[qb] * jnp.concatenate([factor, factor], axis=1)
        for n in range(2):
            weights = jnp.exp(scores[n] - level)
            if masks is not None:
                weights = jnp.where(masks[n], weights, 0.0)
            acc = acc + cdot(weights.astype(BF), values[n])
        acc_ref[qb] = acc
        max_ref[qb] = new

    def pair(i, carry):
        qb = i >> 2
        kb = i & 3
        qi = block((y - qb) & 3, x, c)
        ki = [block((y - kb) & 3, xk, cc) for cc in (c, 1 - c)]
        low = jnp.minimum(ki[0][0], ki[1][0])
        high = jnp.maximum(ki[0][1], ki[1][1])
        meets = jnp.logical_and(qi[1] >= low, qi[0] <= high)
        uniform = jnp.logical_and(jnp.logical_and(qi[0] == qi[1], low == high), qi[0] == low)

        @pl.when(uniform)
        def _():
            update(qb, kb, None)

        @pl.when(jnp.logical_and(meets, jnp.logical_not(uniform)))
        def _():
            rows = row_images(qi, 0)
            update(qb, kb, [rows == row_images(k, 1) for k in ki])

        return carry

    lax.fori_loop(0, 16, pair, 0)
    if last:
        for b in range(4):
            o_ref[b] = (acc_ref[b, :, 0:HD] / acc_ref[b, :, HD : 2 * HD]).astype(BF)


def attend(scalars, q, kv_own, kv_sib, state, last):
    first = state is None
    state_shapes = [
        jax.ShapeDtypeStruct((4, ROWS, 2 * HD), F32),
        jax.ShapeDtypeStruct((4, ROWS, HD), F32),
    ]
    args = [scalars, q, kv_own, kv_sib] + ([] if first else list(state))

    def body(*refs):
        attention_body(first, last, *refs)

    specs = [SMEM] + [VMEM] * (len(args) - 1)
    if last:
        return call(
            body,
            jax.ShapeDtypeStruct((4, ROWS, HD), BF),
            scratch=[pltpu.VMEM(s.shape, s.dtype) for s in state_shapes],
            in_specs=specs,
        )(*args)
    return call(body, state_shapes, in_specs=specs)(*args)


def out_body(s_ref, o0, o1, o2, o3, w0, w1, w2, w3, x_ref, scale_ref, r_ref, stats_ref):
    y = s_ref[0]
    acc = jnp.zeros((ROWS, w0.shape[1]), F32)
    for o_ref, w_ref in ((o0, w0), (o1, w1), (o2, w2), (o3, w3)):
        heads = jnp.concatenate([o_ref[k] for k in range(4)], axis=1)
        rows = jnp.concatenate(
            [w_ref[pl.ds(pl.multiple_of(HD * ((y + k) & 3), HD), HD), :] for k in range(4)], axis=0
        )
        acc = acc + cdot(heads, rows)
    residual = cdot(sub_row_permutation(), x_ref[...]) + scale_ref[...] * acc
    total = jnp.zeros((MROWS, 1), F32)
    squares = jnp.zeros((MROWS, 1), F32)
    for sub in range(4):
        part = residual[MROWS * sub : MROWS * (sub + 1)]
        r_ref[sub] = part
        total = total + jnp.sum(part, axis=1, keepdims=True)
        squares = squares + jnp.sum(part * part, axis=1, keepdims=True)
    lane = lax.broadcasted_iota(jnp.int32, (MROWS, HD), 1)
    stats_ref[...] = jnp.where(lane == 0, total, squares)


def weight_body(s_ref, own_ref, sib_ref, mine_ref, other_ref):
    c = s_ref[0]
    row = lax.broadcasted_iota(jnp.int32, (128, 128), 0)
    col = lax.broadcasted_iota(jnp.int32, (128, 128), 1)
    perm = jnp.where(4 * (row & 31) + (row >> 5) == col, 1.0, 0.0).astype(BF)
    for b in range(own_ref.shape[0] // 128):
        rows = slice(128 * b, 128 * (b + 1))
        own = cdot(perm, own_ref[rows]).astype(BF)
        sib = cdot(perm, sib_ref[rows]).astype(BF)
        both = jnp.concatenate(
            [jnp.where(c == 0, own, sib), jnp.where(c == 0, sib, own)], axis=1
        )
        dest = slice(32 * b, 32 * (b + 1))
        for i in range(2):
            low = both[32 * i : 32 * (i + 1)]
            high = both[64 + 32 * i : 64 + 32 * (i + 1)]
            mine_ref[i, dest] = jnp.where(c == 0, low, high)
            other_ref[i, dest] = jnp.where(c == 0, high, low)


def projection_body(s_ref, a0, a1, a2, a3, *refs):
    weights = refs[:8]
    out_ref, own_ref, w_ref, sems = refs[8:]
    copies = [pltpu.make_async_copy(weights[n], w_ref.at[n], sems.at[n]) for n in range(8)]
    for copy in copies:
        copy.start()
    y, z, c = s_ref[0], s_ref[1], s_ref[2]
    blocks = []
    for base in (2 * c, 2 - 2 * c):
        for i in range(2):
            blocks.append(jnp.concatenate([a[base + i] for a in (a0, a1, a2, a3)], axis=0))
    for k in range(4):
        copies[2 * k].wait()
        acc = cdot(blocks[0], w_ref[2 * k, 0]) + cdot(blocks[1], w_ref[2 * k, 1])
        copies[2 * k + 1].wait()
        acc = acc + cdot(blocks[2], w_ref[2 * k + 1, 0]) + cdot(blocks[3], w_ref[2 * k + 1, 1])
        target = (y - k - z) & 3
        out_ref[target] = acc.astype(BF)

        @pl.when(target == 0)
        def _(acc=acc):
            own_ref[...] = acc


def place_body(s_ref, r0, r1, r2, r3, slots_ref, text_ref, tslots_ref, own_ref, sib_ref):
    y, x, c = s_ref[0], s_ref[1], s_ref[2]

    def positions(core):
        row = lax.broadcasted_iota(jnp.int32, (448, 1), 0)
        k = (row >= 112).astype(jnp.int32) + (row >= 224).astype(jnp.int32) + (row >= 336).astype(jnp.int32)
        return 112 * (8 * y + 2 * ((x + k) & 3) + core) + row - 112 * k

    def pick(position, slots):
        return jnp.where(position == slots, 1.0, 0.0).astype(BF)

    rows = jnp.concatenate([r[...] for r in (r0, r1, r2, r3)], axis=0)
    mine = positions(c)
    own = cdot(pick(mine, slots_ref[...]), rows) + cdot(pick(mine, tslots_ref[...]), text_ref[...])
    own_ref[...] = own.astype(BF)
    sib_ref[...] = cdot(pick(positions(1 - c), slots_ref[...]), rows).astype(BF)


def stream_body(s_ref, b0, b1, b2, b3, out_ref, squares_ref):
    x = s_ref[0]
    width = b0.shape[1]
    total = jnp.zeros((b0.shape[0], 1), F32)
    blocks = [b0[...], b1[...], b2[...], b3[...]]
    for place in range(4):
        k = (x - place) & 3
        value = blocks[0]
        for n in range(1, 4):
            value = jnp.where(k == n, blocks[n], value)
        out_ref[:, width * place : width * (place + 1)] = value
        wide = value.astype(F32)
        total = total + jnp.sum(wide * wide, axis=1, keepdims=True)
    squares_ref[...] = jnp.broadcast_to(total, squares_ref.shape)


def sum_over_z(value):
    return value + shift(value, "z", 1) + shift(value, "z", 2) + shift(value, "z", 3)


def per_device(
    patches,
    norm_gain,
    query_weight,
    key_weight,
    value_weight,
    out_weight,
    layer_scale,
    merge_gain,
    merge_bias,
    proj_weight,
    proj_bias,
    text_rows,
    stream_gain,
    tile_counts,
    image_slots,
    text_slots,
):
    y, x, c, z = [lax.axis_index(name).astype(jnp.int32) for name in ("y", "x", "c", "z")]
    bounds = jnp.cumsum(tile_counts) * 1024
    width = patches.shape[1]
    share = width // 4

    kv, q = project_qkv(
        y[None], patches, norm_gain[None], key_weight, value_weight, query_weight
    )
    kv_own = jnp.stack([kv[0]] + [shift(kv[k], "y", k) for k in (1, 2, 3)])
    q_own = jnp.stack([q[0]] + [shift(q[k], "y", k) for k in (1, 2, 3)])

    state = None
    for step, k in enumerate((0, 1, 3, 2)):
        kv_now = kv_own if k == 0 else shift(kv_own, "x", k)
        scalars = jnp.stack([y, x, c, (x - k) & 3, bounds[0], bounds[1]])
        state = attend(scalars, q_own, kv_now, swap(kv_now), state, step == 3)
    attended = state
    heads = jnp.stack([attended[0]] + [shift(attended[k], "y", 4 - k) for k in (1, 2, 3)])

    columns = jnp.stack([out_weight[:, share * i : share * (i + 1)] for i in range(4)])
    out_parts = [lax.dynamic_index_in_dim(columns, (z + k) & 3, 0, keepdims=False) for k in range(4)]
    out_parts = [out_parts[0]] + [shift(out_parts[k], "z", k) for k in (1, 2, 3)]
    head_parts = [heads] + [shift(heads, "z", k) for k in (1, 2, 3)]
    patch_columns = jnp.stack([patches[:, share * i : share * (i + 1)] for i in range(4)])
    patch_share = lax.dynamic_index_in_dim(patch_columns, z, 0, keepdims=False)
    scale_share = lax.dynamic_index_in_dim(layer_scale.reshape(4, 1, share), z, 0, keepdims=False)
    residual, stats = call(
        out_body,
        (
            jax.ShapeDtypeStruct((4, MROWS, share), F32),
            jax.ShapeDtypeStruct((MROWS, HD), F32),
        ),
        in_specs=[SMEM] + [VMEM] * 10,
    )(y[None], *head_parts, *out_parts, patch_share, scale_share)
    stats = sum_over_z(stats) * (1.0 / (4 * width))
    mean_row = stats[:, 0:1]
    var_row = stats[:, 1:2] - mean_row * mean_row
    gain = merge_gain.reshape(share, 4).T[:, None, :]
    bias = merge_bias.reshape(share, 4).T[:, None, :]
    merged = ((residual - mean_row) * lax.rsqrt(var_row + 1e-05) * gain + bias).astype(BF)

    mine, other = call(
        weight_body,
        (
            jax.ShapeDtypeStruct((2, share, ROWS), BF),
            jax.ShapeDtypeStruct((2, share, ROWS), BF),
        ),
        in_specs=[SMEM, VMEM, VMEM],
    )(c[None], proj_weight, swap(proj_weight))
    weights = [mine, other]
    for k in (1, 2, 3):
        moved = shift(mine, "y", k)
        weights += [moved, swap(moved)]
    merged_parts = [merged] + [shift(merged, "x", k) for k in (1, 2, 3)]
    partial, own_part = call(
        projection_body,
        (
            jax.ShapeDtypeStruct((4, ROWS, ROWS), BF),
            jax.ShapeDtypeStruct((ROWS, ROWS), F32),
        ),
        scratch=[pltpu.VMEM((8, 2, share, ROWS), BF), pltpu.SemaphoreType.DMA((8,))],
        in_specs=[SMEM] + [VMEM] * 4 + [ANY] * 8,
    )(jnp.stack([y, z, c]), *merged_parts, *weights)
    summed = own_part
    for k in (1, 2, 3):
        summed = summed + shift(partial[k], "z", k).astype(F32)

    turn = [(4 * a + b, 4 * b + a) for a in range(4) for b in range(4)]

    def both_cores(value):
        value = lax.ppermute(value, ("y", "z"), turn)
        sibling = swap(value)
        return jnp.where(
            c == 0,
            jnp.concatenate([value, sibling], axis=1),
            jnp.concatenate([sibling, value], axis=1),
        )

    text = both_cores(text_rows)
    bias_row = both_cores(proj_bias[None])
    rows = jax.nn.gelu(summed + bias_row, approximate=False).astype(BF)

    row_parts = [rows] + [shift(rows, "y", k) for k in (1, 2, 3)]
    order = jnp.arange(4, dtype=jnp.int32)
    slots = image_slots.reshape(4, 4, 2, MROWS)
    slots = lax.dynamic_index_in_dim(slots, c, 2, keepdims=False)
    slots = slots[(y - order) & 3][:, (x - order) & 3].reshape(1, 16 * MROWS)
    placed, for_sibling = call(
        place_body,
        (
            jax.ShapeDtypeStruct((448, ROWS), BF),
            jax.ShapeDtypeStruct((448, ROWS), BF),
        ),
        in_specs=[SMEM] + [VMEM] * 7,
    )(jnp.stack([y, x, c]), *row_parts, slots, text, text_slots[None])
    placed = (placed + swap(for_sibling)).reshape(4, 112, ROWS)
    blocks = [placed[0]] + [shift(placed[k], "x", k) for k in (1, 2, 3)]
    stream, squares = call(
        stream_body,
        (
            jax.ShapeDtypeStruct((112, 4 * ROWS), BF),
            jax.ShapeDtypeStruct((112, HD), F32),
        ),
        in_specs=[SMEM] + [VMEM] * 4,
    )(x[None], *blocks)
    squares = sum_over_z(squares)[:, 0:1]
    inverse_rms = lax.rsqrt(squares * (1.0 / 6144) + 1e-05)
    normed = (stream.astype(F32) * inverse_rms * stream_gain).astype(BF)
    return (stream, normed)


def solution(mesh):
    grid = Mesh(mesh.devices.reshape(4, 4, 2, 4), ("y", "x", "c", "z"))
    seq = ("y", "x", "c")
    return jax.shard_map(
        per_device,
        mesh=grid,
        in_specs=(
            P(seq, None),
            P(),
            P(None, "z"),
            P(None, "z"),
            P(None, "z"),
            P("z", None),
            P(),
            P("z"),
            P("z"),
            P("z", seq),
            P(seq),
            P(None, seq),
            P("z"),
            P(),
            P(),
            P(),
        ),
        out_specs=(P(seq, "z"), P(seq, "z")),
        check_vma=False,
    )
```

```python
import jax
import jax.numpy as jnp
from jax import lax
from jax.experimental import pallas as pl
from jax.experimental.pallas import tpu as pltpu
from jax.sharding import Mesh, PartitionSpec as P

HD = 128
ROWS = 384
MROWS = 96
BF = jnp.bfloat16
F32 = jnp.float32
LIMIT = 60 * 1024 * 1024


def cdot(a, b):
    return jnp.dot(a, b, preferred_element_type=F32)


def shift(value, axis, k):
    return lax.ppermute(value, axis, [(i, (i + k) % 4) for i in range(4)])


def swap(value):
    return lax.ppermute(value, "c", [(0, 1), (1, 0)])


def cost(us):
    return pl.CostEstimate(flops=int(us * 1.0e9), transcendentals=0, bytes_accessed=0)


def call(body, out_shape, us, scratch=(), **kw):
    return pl.pallas_call(
        body,
        out_shape=out_shape,
        scratch_shapes=scratch,
        cost_estimate=cost(us),
        compiler_params=pltpu.CompilerParams(vmem_limit_bytes=LIMIT),
        **kw,
    )


SMEM = pl.BlockSpec(memory_space=pltpu.SMEM)
VMEM = pl.BlockSpec(memory_space=pltpu.VMEM)
ANY = pl.BlockSpec(memory_space=pl.ANY)


def sub_row_permutation():
    row = lax.broadcasted_iota(jnp.int32, (ROWS, ROWS), 0)
    col = lax.broadcasted_iota(jnp.int32, (ROWS, ROWS), 1)
    sub = (row >= 96).astype(jnp.int32) + (row >= 192).astype(jnp.int32) + (row >= 288).astype(jnp.int32)
    m = row - 96 * sub
    source = (2 * (m >> 4) + (sub >> 1)) * 32 + 2 * (m & 15) + (sub & 1)
    return jnp.where(source == col, 1.0, 0.0).astype(BF)


def qkv_body(s_ref, x_ref, g_ref, wk_ref, wv_ref, wq_ref, kvq_ref, xn_ref):
    half = pl.program_id(0)

    @pl.when(half == 0)
    def _():
        xf = cdot(sub_row_permutation(), x_ref[...])
        scale = lax.rsqrt(jnp.mean(xf * xf, axis=-1, keepdims=True) + 1e-06)
        xn_ref[...] = (xf * scale * g_ref[...]).astype(BF)

    xn = xn_ref[...]
    keys = cdot(xn, wk_ref[...]).astype(BF)
    values = cdot(xn, wv_ref[...]).astype(BF)
    queries = (cdot(xn, wq_ref[...]) * HD ** (-0.5)).astype(BF)
    for i in range(2):
        slot = (2 * half + i - s_ref[0]) & 3
        part = slice(HD * i, HD * (i + 1))
        kvq_ref[slot, :, 0:HD] = keys[:, part]
        kvq_ref[slot, :, HD : 2 * HD] = values[:, part]
        kvq_ref[slot, :, 2 * HD : 3 * HD] = queries[:, part]


def project_qkv(y, patches, gain, wk, wv, wq):
    width = patches.shape[1]
    whole = pl.BlockSpec((ROWS, width), lambda j, s: (0, 0))
    weight = pl.BlockSpec((width, 2 * HD), lambda j, s: (0, j))
    return pl.pallas_call(
        qkv_body,
        out_shape=jax.ShapeDtypeStruct((4, ROWS, 3 * HD), BF),
        grid_spec=pltpu.PrefetchScalarGridSpec(
            num_scalar_prefetch=1,
            grid=(2,),
            in_specs=[whole, pl.BlockSpec((1, width), lambda j, s: (0, 0)), weight, weight, weight],
            out_specs=pl.BlockSpec((4, ROWS, 3 * HD), lambda j, s: (0, 0, 0)),
            scratch_shapes=[pltpu.VMEM((ROWS, width), BF)],
        ),
        cost_estimate=cost(11),
        compiler_params=pltpu.CompilerParams(
            dimension_semantics=("arbitrary",), vmem_limit_bytes=LIMIT
        ),
    )(y, patches, gain, wk, wv, wq)


def image_lanes(info, scale, same):
    row = lax.broadcasted_iota(jnp.int32, (ROWS, HD), 0)
    lane = lax.broadcasted_iota(jnp.int32, (ROWS, HD), 1)
    sub = (row >= 96).astype(jnp.int32) + (row >= 192).astype(jnp.int32) + (row >= 288).astype(jnp.int32)
    image = jnp.where((row - 96 * sub) * 4 < info[2], info[0], info[1])
    hit = lane == image if same else lane != image
    return jnp.where(hit, scale, 0.0).astype(BF)


def attention_body(steps, first, last, s_ref, t_ref, q_ref, *refs):
    rest = refs[:-2]
    own_ref, sib_ref = refs[-2:]
    filled = 0
    while filled < len(steps):
        own, sib = rest[:2]
        rest = rest[2:]
        own_ref[filled : filled + own.shape[0]] = own[...]
        sib_ref[filled : filled + own.shape[0]] = sib[...]
        filled += own.shape[0]
    if not first:
        acc_in, max_in = rest[:2]
        rest = rest[2:]
    if last:
        o_ref, acc_ref, max_ref = rest
    else:
        acc_ref, max_ref = rest
    if first:
        acc_ref[...] = jnp.zeros(acc_ref.shape, F32)
        max_ref[...] = jnp.full(max_ref.shape, -1e30, F32)
    else:
        acc_ref[...] = acc_in[...]
        max_ref[...] = max_in[...]
    y, x, c = s_ref[0], s_ref[1], s_ref[2]
    bound0 = 1024 * t_ref[0]
    bound1 = 1024 * (t_ref[0] + t_ref[1])

    def image_of(row):
        return (row >= bound0).astype(jnp.int32) + (row >= bound1).astype(jnp.int32)

    def block(yy, xx, cc):
        base = ROWS * (8 * yy + 2 * xx + cc)
        return image_of(base), image_of(base + ROWS - 1), 1024 - (base & 1023)

    def update(qb, kr, qi, ki):
        marks = image_lanes(qi, -1e30, False)
        keys, values = [], []
        for n, ref in enumerate((own_ref, sib_ref)):
            keys.append(jnp.concatenate([ref[kr, :, 0:HD], image_lanes(ki[n], 1.0, True)], axis=1))
            values.append(
                jnp.concatenate([ref[kr, :, HD : 2 * HD], jnp.ones((ROWS, HD), BF)], axis=1)
            )
        keys = jnp.concatenate(keys, axis=0)
        values = jnp.concatenate(values, axis=0)
        half = ROWS // 2

        def score(rows):
            q = jnp.concatenate([q_ref[qb, rows, :], marks[rows]], axis=1)
            return lax.dot_general(q, keys, (((1,), (1,)), ((), ())), preferred_element_type=F32)

        def fold(rows, scores):
            old = max_ref[qb, rows]
            new = jnp.maximum(old, jnp.max(scores, axis=1, keepdims=True))
            factor = jnp.exp(old - new)
            weights = jnp.exp(scores - new[:, 0:1]).astype(BF)
            acc = acc_ref[qb, rows] * jnp.concatenate([factor, factor], axis=1)
            acc_ref[qb, rows] = acc + cdot(weights, values)
            max_ref[qb, rows] = new

        upper, lower = slice(0, half), slice(half, ROWS)
        first_scores = score(upper)
        second_scores = score(lower)
        fold(upper, first_scores)
        fold(lower, second_scores)

    def pair(i, carry):
        qb = i & 3
        kr = i >> 2
        qi = block((y - qb) & 3, x, c)
        step = steps[0] if len(steps) == 4 else jnp.where(kr < 4, steps[0], steps[4])
        xk = (x - step) & 3
        ki = [block((y - kr) & 3, xk, cc) for cc in (c, 1 - c)]
        low = jnp.minimum(ki[0][0], ki[1][0])
        high = jnp.maximum(ki[0][1], ki[1][1])

        @pl.when(jnp.logical_and(qi[1] >= low, qi[0] <= high))
        def _():
            update(qb, kr, qi, ki)

        return carry

    lax.fori_loop(0, 4 * len(steps), pair, 0)
    if last:
        for b in range(4):
            o_ref[b] = (acc_ref[b, :, 0:HD] / acc_ref[b, :, HD : 2 * HD]).astype(BF)


def attend(steps, coords, tile_counts, q, blocks, state, last):
    first = state is None
    state_shapes = [
        jax.ShapeDtypeStruct((4, ROWS, 2 * HD), F32),
        jax.ShapeDtypeStruct((4, ROWS, HD), F32),
    ]
    args = [coords, tile_counts, q, *blocks] + ([] if first else list(state))

    def body(*refs):
        attention_body(steps, first, last, *refs)

    specs = [SMEM, SMEM] + [VMEM] * (len(args) - 2)
    held = [pltpu.VMEM((len(steps), ROWS, 2 * HD), BF)] * 2
    if last:
        return call(
            body,
            jax.ShapeDtypeStruct((4, ROWS, HD), BF),
            2.5 * len(steps),
            scratch=[pltpu.VMEM(s.shape, s.dtype) for s in state_shapes] + held,
            in_specs=specs,
        )(*args)
    return call(body, state_shapes, 2.5 * len(steps), scratch=held, in_specs=specs)(*args)


def pack_body(m0, m1, m2, m3, kv_ref, q_ref):
    for k, ref in enumerate((m0, m1, m2, m3)):
        kv_ref[k] = ref[:, 0 : 2 * HD]
        q_ref[k] = ref[:, 2 * HD : 3 * HD]


def turn_body(gain_ref, bias_ref, out_ref):
    out_ref[0:4] = gain_ref[...].T
    out_ref[4:8] = bias_ref[...].T


WINDOW = 896


def window(z):
    return pl.ds(pl.multiple_of(768 * z, HD), WINDOW)


def window_body(w_ref, out_ref):
    for i in range(4):
        out_ref[i] = w_ref[:, 768 * i : 768 * i + WINDOW]


def out_body(s_ref, o0, o1, o2a, o2b, o3, weight, x_any, scale_ref, r_ref, stats_ref, w_ref, x_ref, sems):
    y, z = s_ref[0], s_ref[3]
    copies = [
        pltpu.make_async_copy(weight, w_ref, sems.at[0]),
        pltpu.make_async_copy(x_any.at[:, window(z)], x_ref, sems.at[1]),
    ]
    for copy in copies:
        copy.start()
    acc = jnp.zeros((ROWS, WINDOW), F32)
    for copy in copies:
        copy.wait()
    parts = [
        [o0[k] for k in range(4)],
        [o1[k] for k in range(4)],
        [o2a[0], o2a[1], o2b[0], o2b[1]],
        [o3[k] for k in range(4)],
    ]
    for j in range(4):
        heads = jnp.concatenate(parts[j], axis=1)
        plane = (z - j) & 3
        rows = jnp.concatenate(
            [w_ref[plane, pl.ds(pl.multiple_of(HD * ((y + k) & 3), HD), HD), :] for k in range(4)],
            axis=0,
        )
        acc = acc + cdot(heads, rows)
    residual = cdot(sub_row_permutation(), x_ref[...]) + scale_ref[:, window(z)] * acc
    residual = pltpu.roll(residual, WINDOW - 32 * z, 1)[:, 0 : r_ref.shape[2]]
    total = jnp.zeros((MROWS, 1), F32)
    squares = jnp.zeros((MROWS, 1), F32)
    for sub in range(4):
        part = residual[MROWS * sub : MROWS * (sub + 1)]
        r_ref[sub] = part
        total = total + jnp.sum(part, axis=1, keepdims=True)
        squares = squares + jnp.sum(part * part, axis=1, keepdims=True)
    lane = lax.broadcasted_iota(jnp.int32, (MROWS, HD), 1)
    stats_ref[...] = jnp.where(lane == 0, total, squares)


def merge_body(stats_ref, r_ref, affine_ref, out_ref):
    share = r_ref.shape[2]
    stats = stats_ref[...] * (1.0 / (16 * share))
    mean = stats[:, 0:1]
    scale = lax.rsqrt(stats[:, 1:2] - mean * mean + 1e-05)
    for sub in range(4):
        gain, bias = affine_ref[sub : sub + 1], affine_ref[4 + sub : 5 + sub]
        value = (r_ref[sub] - mean) * scale * gain + bias
        out_ref[:, share * sub : share * (sub + 1)] = value.astype(BF)


def weight_body(s_ref, own_ref, sib_ref, mine_ref, other_ref):
    c = s_ref[2]
    row = lax.broadcasted_iota(jnp.int32, (128, 128), 0)
    col = lax.broadcasted_iota(jnp.int32, (128, 128), 1)
    perm = jnp.where(4 * (row & 31) + (row >> 5) == col, 1.0, 0.0).astype(BF)
    share = own_ref.shape[1] // 4

    def reorder(ref, rows):
        return lax.dot_general(
            perm, ref[:, rows], (((1,), (1,)), ((), ())), preferred_element_type=F32
        ).astype(BF)

    for b in range(own_ref.shape[1] // 128):
        rows = slice(128 * b, 128 * (b + 1))
        own = reorder(own_ref, rows)
        sib = reorder(sib_ref, rows)
        both = jnp.concatenate(
            [jnp.where(c == 0, own, sib), jnp.where(c == 0, sib, own)], axis=1
        )
        for i in range(2):
            dest = slice(share * i + 32 * b, share * i + 32 * (b + 1))
            low = both[32 * i : 32 * (i + 1)]
            high = both[64 + 32 * i : 64 + 32 * (i + 1)]
            mine_ref[dest, :] = jnp.where(c == 0, low, high)
            other_ref[dest, :] = jnp.where(c == 0, high, low)


def projection_body(rels, s_ref, a0, a1, a2a, a2b, a3, mine, other, *refs):
    outs = refs[: len(rels)]
    a_ref, w_ref = refs[len(rels) :]
    x, c, z = s_ref[1], s_ref[2], s_ref[3]
    half = mine.shape[1]

    def rows(j, offset, count):
        return pl.ds(pl.multiple_of(MROWS * ((x - j) & 3) + offset, 16), count)

    a_ref[rows(0, 0, 96), :] = a0[...]
    a_ref[rows(1, 0, 96), :] = a1[...]
    a_ref[rows(2, 0, 48), :] = a2a[...]
    a_ref[rows(2, 48, 48), :] = a2b[...]
    a_ref[rows(3, 0, 96), :] = a3[...]
    for n, rel in enumerate(rels):
        columns = slice(ROWS * n, ROWS * (n + 1))
        k = (z + rel) & 3
        w_ref[pl.ds(pl.multiple_of(half * c, 64), half), columns] = mine[k]
        w_ref[pl.ds(pl.multiple_of(half * (1 - c), 64), half), columns] = other[k]
    acc = cdot(a_ref[...], w_ref[...])
    for n in range(len(rels)):
        outs[n][...] = acc[:, ROWS * n : ROWS * (n + 1)].astype(outs[n].dtype)


def place_body(s_ref, r0, r1, r2a, r2b, r3, slots_ref, text_ref, tslots_ref, own_ref, sib_ref, rows_ref):
    y, x, c = s_ref[0], s_ref[1], s_ref[2]

    def positions(core):
        row = lax.broadcasted_iota(jnp.int32, (448, 1), 0)
        k = (row >= 112).astype(jnp.int32) + (row >= 224).astype(jnp.int32) + (row >= 336).astype(jnp.int32)
        return 112 * (8 * y + 2 * ((x + k) & 3) + core) + row - 112 * k

    def pick(position, slots):
        return jnp.where(position == slots, 1.0, 0.0).astype(BF)

    for k, offset, r in ((0, 0, r0), (1, 0, r1), (2, 0, r2a), (2, 192, r2b), (3, 0, r3)):
        start = pl.multiple_of(ROWS * ((y - k) & 3) + offset, 64)
        rows_ref[pl.ds(start, r.shape[0]), :] = r[...]
    rows = rows_ref[...]
    mine = positions(c)
    own = cdot(pick(mine, slots_ref[...]), rows) + cdot(pick(mine, tslots_ref[...]), text_ref[...])
    own_ref[...] = own.astype(BF)
    sib_ref[...] = cdot(pick(positions(1 - c), slots_ref[...]), rows).astype(BF)


def stream_body(s_ref, b0, b1, b2, b3, out_ref, squares_ref):
    x = s_ref[1]
    width = b0.shape[1]
    total = jnp.zeros((b0.shape[0], 1), F32)
    blocks = [b0[...], b1[...], b2[...], b3[...]]
    for place in range(4):
        k = (x - place) & 3
        value = blocks[0]
        for n in range(1, 4):
            value = jnp.where(k == n, blocks[n], value)
        out_ref[:, width * place : width * (place + 1)] = value
        wide = value.astype(F32)
        total = total + jnp.sum(wide * wide, axis=1, keepdims=True)
    squares_ref[...] = jnp.broadcast_to(total, squares_ref.shape)


def after(values):
    return lax.optimization_barrier(values)


def sum_over_z(value):
    value = value + lax.ppermute(value, "z", [(i, i ^ 1) for i in range(4)])
    return value + lax.ppermute(value, "z", [(i, i ^ 2) for i in range(4)])


def ring(value, axis):
    half = value.shape[0] // 2
    back = shift(value, axis, 1)
    ahead = shift(value, axis, 3)
    return [value, back, shift(back[:half], axis, 1), shift(ahead[half:], axis, 3), ahead]


def per_device(
    patches,
    norm_gain,
    query_weight,
    key_weight,
    value_weight,
    out_weight,
    layer_scale,
    merge_gain,
    merge_bias,
    proj_weight,
    proj_bias,
    text_rows,
    stream_gain,
    tile_counts,
    image_slots,
    text_slots,
):
    y, x, c, z = [lax.axis_index(name).astype(jnp.int32) for name in ("y", "x", "c", "z")]
    coords = jnp.stack([y, x, c, z])
    width = patches.shape[1]
    share = width // 4

    kvq = project_qkv(coords, patches, norm_gain[None], key_weight, value_weight, query_weight)

    turn = [(4 * a + b, 4 * b + a) for a in range(4) for b in range(4)]

    def both_cores(value):
        value = lax.ppermute(value, ("y", "z"), turn)
        sibling = swap(value)
        return jnp.where(
            c == 0,
            jnp.concatenate([value, sibling], axis=1),
            jnp.concatenate([sibling, value], axis=1),
        )

    proj_turned = proj_weight.T
    kvq, out_weight, proj_turned, proj_sibling = after(
        (kvq, out_weight, proj_turned, swap(proj_turned))
    )
    moved = [kvq[0]] + [shift(kvq[k], "y", k) for k in (1, 2, 3)]
    windows = call(
        window_body,
        jax.ShapeDtypeStruct((4, out_weight.shape[0], WINDOW), BF),
        0.1,
        in_specs=[VMEM],
    )(out_weight)
    mine, other = call(
        weight_body,
        (
            jax.ShapeDtypeStruct((2 * share, ROWS), BF),
            jax.ShapeDtypeStruct((2 * share, ROWS), BF),
        ),
        0.1,
        in_specs=[SMEM, VMEM, VMEM],
    )(coords, proj_turned, proj_sibling)
    out_parts = lax.all_to_all(windows, "z", 0, 0, tiled=True)
    gathered = lax.all_gather(mine, "y", axis=0)
    windows, mine, *moved = after((windows, mine, *moved))
    kv_own, q_own = call(
        pack_body,
        (
            jax.ShapeDtypeStruct((4, ROWS, 2 * HD), BF),
            jax.ShapeDtypeStruct((4, ROWS, HD), BF),
        ),
        1,
        in_specs=[VMEM] * 4,
    )(*moved)
    near = [shift(kv_own, "x", 1), shift(kv_own, "x", 3)]
    kv_sib = swap(kv_own)

    where = (coords, tile_counts, q_own)
    state = attend((0,) * 4, *where, [kv_own, kv_sib], None, False)
    near, state = after((near, state))
    far = [shift(near[0][0:2], "x", 1), shift(near[1][2:4], "x", 3)]
    blocks = [near[0], swap(near[0]), near[1], swap(near[1])]
    state = attend((1,) * 4 + (3,) * 4, *where, blocks, state, False)
    far, state, out_parts = after((far, state, out_parts))
    blocks = [far[0], swap(far[0]), far[1], swap(far[1])]
    attended = attend((2,) * 4, *where, blocks, state, True)
    heads = jnp.stack([attended[0]] + [shift(attended[k], "y", 4 - k) for k in (1, 2, 3)])
    gathered, other, heads, merge_gain, merge_bias, layer_scale = after(
        (gathered, other, heads, merge_gain, merge_bias, layer_scale)
    )

    head_parts = ring(heads, "z")
    other_gathered = swap(gathered)
    affine = call(
        turn_body, jax.ShapeDtypeStruct((8, share), F32), 1, in_specs=[VMEM] * 2
    )(merge_gain.reshape(share, 4), merge_bias.reshape(share, 4))
    *head_parts, affine = after((*head_parts, affine))
    residual, stats = call(
        out_body,
        (
            jax.ShapeDtypeStruct((4, MROWS, share), F32),
            jax.ShapeDtypeStruct((MROWS, HD), F32),
        ),
        6,
        scratch=[
            pltpu.VMEM((4, 4 * HD, WINDOW), BF),
            pltpu.VMEM((ROWS, WINDOW), BF),
            pltpu.SemaphoreType.DMA((2,)),
        ],
        in_specs=[SMEM] + [VMEM] * 5 + [ANY] * 2 + [VMEM],
    )(coords, *head_parts, out_parts, patches, layer_scale[None])
    merged = call(
        merge_body, jax.ShapeDtypeStruct((MROWS, width), BF), 1, in_specs=[VMEM] * 3
    )(sum_over_z(stats), residual, affine)

    merged_parts = ring(merged, "x")
    merged, text_rows, proj_bias, image_slots = after((merged, text_rows, proj_bias, image_slots))
    slots = image_slots.reshape(4, 4, 2, MROWS)
    slots = jnp.where(c == 0, slots[:, :, 0], slots[:, :, 1]).reshape(1, 16 * MROWS)
    text = both_cores(text_rows)
    bias_row = both_cores(proj_bias[None])
    *merged_parts, slots, text, bias_row = after((*merged_parts, slots, text, bias_row))

    def project(rels, types):
        return call(
            lambda *refs: projection_body(rels, *refs),
            [jax.ShapeDtypeStruct((ROWS, ROWS), kind) for kind in types],
            5,
            scratch=[pltpu.VMEM((ROWS, width), BF), pltpu.VMEM((width, 2 * ROWS), BF)],
            in_specs=[SMEM] + [VMEM] * 7,
        )(coords, *merged_parts, gathered, other_gathered)

    partial = [None] * 4
    partial[2], partial[1] = project((2, 1), (BF, BF))
    partial[3], summed = project((3, 0), (BF, F32))
    for k in (1, 2, 3):
        summed = summed + shift(partial[k], "z", k).astype(F32)

    rows = jax.nn.gelu(summed + bias_row, approximate=False).astype(BF)

    row_parts = ring(rows, "y")
    placed, for_sibling = call(
        place_body,
        (
            jax.ShapeDtypeStruct((448, ROWS), BF),
            jax.ShapeDtypeStruct((448, ROWS), BF),
        ),
        4,
        scratch=[pltpu.VMEM((4 * ROWS, ROWS), BF)],
        in_specs=[SMEM] + [VMEM] * 8,
    )(coords, *row_parts, slots, text, text_slots[None])
    placed = (placed + swap(for_sibling)).reshape(4, 112, ROWS)
    blocks = [placed[0]] + [shift(placed[k], "x", k) for k in (1, 2, 3)]
    stream, squares = call(
        stream_body,
        (
            jax.ShapeDtypeStruct((112, 4 * ROWS), BF),
            jax.ShapeDtypeStruct((112, HD), F32),
        ),
        2,
        in_specs=[SMEM] + [VMEM] * 4,
    )(coords, *blocks)
    squares = sum_over_z(squares)[:, 0:1]
    inverse_rms = lax.rsqrt(squares * (1.0 / 6144) + 1e-05)
    normed = (stream.astype(F32) * inverse_rms * stream_gain).astype(BF)
    return (stream, normed)


def solution(mesh):
    grid = Mesh(mesh.devices.reshape(4, 4, 2, 4), ("y", "x", "c", "z"))
    seq = ("y", "x", "c")
    return jax.shard_map(
        per_device,
        mesh=grid,
        in_specs=(
            P(seq, None),
            P(),
            P(None, "z"),
            P(None, "z"),
            P(None, "z"),
            P("z", None),
            P(),
            P("z"),
            P("z"),
            P("z", seq),
            P(seq),
            P(None, seq),
            P("z"),
            P(),
            P(),
            P(),
        ),
        out_specs=(P(seq, "z"), P(seq, "z")),
        check_vma=False,
    )
```

```python
import jax
import jax.numpy as jnp
from jax import lax
from jax.experimental import pallas as pl
from jax.experimental.pallas import tpu as pltpu
from jax.sharding import Mesh, PartitionSpec as P

HD = 128
ROWS = 384
MROWS = 96
BF = jnp.bfloat16
F32 = jnp.float32
LIMIT = 60 * 1024 * 1024


def cdot(a, b):
    return jnp.dot(a, b, preferred_element_type=F32)


def shift(value, axis, k):
    return lax.ppermute(value, axis, [(i, (i + k) % 4) for i in range(4)])


def swap(value):
    return lax.ppermute(value, "c", [(0, 1), (1, 0)])


def cost(us):
    return pl.CostEstimate(flops=int(us * 1.0e9), transcendentals=0, bytes_accessed=0)


def call(body, out_shape, us, scratch=(), **kw):
    return pl.pallas_call(
        body,
        out_shape=out_shape,
        scratch_shapes=scratch,
        cost_estimate=cost(us),
        compiler_params=pltpu.CompilerParams(vmem_limit_bytes=LIMIT),
        **kw,
    )


SMEM = pl.BlockSpec(memory_space=pltpu.SMEM)
VMEM = pl.BlockSpec(memory_space=pltpu.VMEM)
ANY = pl.BlockSpec(memory_space=pl.ANY)


def sub_row_permutation():
    row = lax.broadcasted_iota(jnp.int32, (ROWS, ROWS), 0)
    col = lax.broadcasted_iota(jnp.int32, (ROWS, ROWS), 1)
    sub = (row >= 96).astype(jnp.int32) + (row >= 192).astype(jnp.int32) + (row >= 288).astype(jnp.int32)
    m = row - 96 * sub
    source = (2 * (m >> 4) + (sub >> 1)) * 32 + 2 * (m & 15) + (sub & 1)
    return jnp.where(source == col, 1.0, 0.0).astype(BF)


def qkv_body(s_ref, x_ref, g_ref, wk_ref, wv_ref, wq_ref, o0, o1, o2, o3, xn_ref):
    half = pl.program_id(0)

    @pl.when(half == 0)
    def _():
        xf = cdot(sub_row_permutation(), x_ref[...])
        scale = lax.rsqrt(jnp.mean(xf * xf, axis=-1, keepdims=True) + 1e-06)
        gain = jnp.concatenate([g_ref[i : i + 1] for i in range(g_ref.shape[0])], axis=1)
        xn_ref[...] = (xf * scale * gain).astype(BF)

    xn = xn_ref[...]
    keys = cdot(xn, wk_ref[...]).astype(BF)
    values = cdot(xn, wv_ref[...]).astype(BF)
    queries = (cdot(xn, wq_ref[...]) * HD ** (-0.5)).astype(BF)
    for i in range(2):
        slot = (2 * half + i - s_ref[0]) & 3
        part = slice(HD * i, HD * (i + 1))
        head = jnp.concatenate([keys[:, part], values[:, part], queries[:, part]], axis=1)
        for k, ref in enumerate((o0, o1, o2, o3)):

            @pl.when(slot == k)
            def _(ref=ref, head=head):
                ref[...] = head


def project_qkv(y, patches, gain, wk, wv, wq):
    width = patches.shape[1]
    whole = pl.BlockSpec((ROWS, width), lambda j, s: (0, 0))
    weight = pl.BlockSpec((width, 2 * HD), lambda j, s: (0, j))
    return pl.pallas_call(
        qkv_body,
        out_shape=[jax.ShapeDtypeStruct((ROWS, 3 * HD), BF)] * 4,
        grid_spec=pltpu.PrefetchScalarGridSpec(
            num_scalar_prefetch=1,
            grid=(2,),
            in_specs=[whole, pl.BlockSpec((width // HD, HD), lambda j, s: (0, 0)), weight, weight, weight],
            out_specs=[pl.BlockSpec((ROWS, 3 * HD), lambda j, s: (0, 0))] * 4,
            scratch_shapes=[pltpu.VMEM((ROWS, width), BF)],
        ),
        cost_estimate=cost(11),
        compiler_params=pltpu.CompilerParams(
            dimension_semantics=("arbitrary",), vmem_limit_bytes=LIMIT
        ),
    )(y, patches, gain, wk, wv, wq)


def image_lanes(info, scale, same):
    row = lax.broadcasted_iota(jnp.int32, (ROWS, HD), 0)
    lane = lax.broadcasted_iota(jnp.int32, (ROWS, HD), 1)
    sub = (row >= 96).astype(jnp.int32) + (row >= 192).astype(jnp.int32) + (row >= 288).astype(jnp.int32)
    image = jnp.where((row - 96 * sub) * 4 < info[2], info[0], info[1])
    hit = lane == image if same else lane != image
    return jnp.where(hit, scale, 0.0).astype(BF)


def attention_body(steps, first, last, s_ref, t_ref, q_ref, *refs):
    rest = refs[:-3]
    own_ref, sib_ref, list_ref = refs[-3:]
    filled = 0
    while filled < len(steps):
        own, sib = rest[:2]
        rest = rest[2:]
        own_ref[filled : filled + own.shape[0]] = own[...]
        sib_ref[filled : filled + own.shape[0]] = sib[...]
        filled += own.shape[0]
    if not first:
        acc_in, max_in = rest[:2]
        rest = rest[2:]
    if last:
        *o_refs, acc_ref, max_ref = rest
    else:
        acc_ref, max_ref = rest
    if first:
        acc_ref[...] = jnp.zeros(acc_ref.shape, F32)
        max_ref[...] = jnp.full(max_ref.shape, -1e30, F32)
    else:
        acc_ref[...] = acc_in[...]
        max_ref[...] = max_in[...]
    y, x, c = s_ref[0], s_ref[1], s_ref[2]
    bound0 = 1024 * t_ref[0]
    bound1 = 1024 * (t_ref[0] + t_ref[1])

    def image_of(row):
        return (row >= bound0).astype(jnp.int32) + (row >= bound1).astype(jnp.int32)

    def block(yy, xx, cc):
        base = ROWS * (8 * yy + 2 * xx + cc)
        return image_of(base), image_of(base + ROWS - 1), 1024 - (base & 1023)

    def blocks_of(i):
        qb = i & 3
        kr = i >> 2
        step = steps[0] if len(steps) == 4 else jnp.where(kr < 4, steps[0], steps[4])
        xk = (x - step) & 3
        ki = [block((y - kr) & 3, xk, cc) for cc in (c, 1 - c)]
        return qb, kr, block((y - qb) & 3, x, c), ki

    def note(i, count):
        qb, kr, qi, ki = blocks_of(i)
        low = jnp.minimum(ki[0][0], ki[1][0])
        high = jnp.maximum(ki[0][1], ki[1][1])
        meets = jnp.logical_and(qi[1] >= low, qi[0] <= high)
        list_ref[count] = i
        return count + meets.astype(jnp.int32)

    def score(i, live):
        qb, kr, qi, ki = blocks_of(i)
        qi = (jnp.where(live, qi[0], 99), jnp.where(live, qi[1], 99), qi[2])
        q = jnp.concatenate([q_ref[qb], image_lanes(qi, -1e30, False)], axis=1)
        keys, values = [], []
        for n, ref in enumerate((own_ref, sib_ref)):
            keys.append(jnp.concatenate([ref[kr, :, 0:HD], image_lanes(ki[n], 1.0, True)], axis=1))
            values.append(
                jnp.concatenate([ref[kr, :, HD : 2 * HD], jnp.ones((ROWS, HD), BF)], axis=1)
            )
        scores = lax.dot_general(
            q, jnp.concatenate(keys, axis=0), (((1,), (1,)), ((), ())), preferred_element_type=F32
        )
        return qb, scores, jnp.concatenate(values, axis=0)

    def fold(qb, scores, values):
        old = max_ref[qb]
        new = jnp.maximum(old, jnp.max(scores, axis=1, keepdims=True))
        factor = jnp.exp(old - new)
        weights = jnp.exp(scores - new[:, 0:1]).astype(BF)
        max_ref[qb] = new
        acc_ref[qb] = acc_ref[qb] * jnp.concatenate([factor, factor], axis=1) + cdot(weights, values)

    def two(t, carry):
        odd = 2 * t + 1 < count
        one = score(list_ref[2 * t], True)
        other = score(list_ref[jnp.where(odd, 2 * t + 1, 2 * t)], odd)
        fold(*one)
        fold(*other)
        return carry

    count = lax.fori_loop(0, 4 * len(steps), note, jnp.int32(0))
    lax.fori_loop(0, (count + 1) >> 1, two, 0)
    if last:
        for b in range(4):
            o_refs[b][...] = (acc_ref[b, :, 0:HD] / acc_ref[b, :, HD : 2 * HD]).astype(BF)


def attend(steps, coords, tile_counts, q, blocks, state, last):
    first = state is None
    state_shapes = [
        jax.ShapeDtypeStruct((4, ROWS, 2 * HD), F32),
        jax.ShapeDtypeStruct((4, ROWS, HD), F32),
    ]
    args = [coords, tile_counts, q, *blocks] + ([] if first else list(state))

    def body(*refs):
        attention_body(steps, first, last, *refs)

    specs = [SMEM, SMEM] + [VMEM] * (len(args) - 2)
    held = [pltpu.VMEM((len(steps), ROWS, 2 * HD), BF)] * 2 + [pltpu.SMEM((64,), jnp.int32)]
    if last:
        return call(
            body,
            [jax.ShapeDtypeStruct((ROWS, HD), BF)] * 4,
            2.5 * len(steps),
            scratch=[pltpu.VMEM(s.shape, s.dtype) for s in state_shapes] + held,
            in_specs=specs,
        )(*args)
    return call(body, state_shapes, 2.5 * len(steps), scratch=held, in_specs=specs)(*args)


def pack_body(m0, m1, m2, m3, kv_ref, q_ref):
    for k, ref in enumerate((m0, m1, m2, m3)):
        kv_ref[k] = ref[:, 0 : 2 * HD]
        q_ref[k] = ref[:, 2 * HD : 3 * HD]


def turn_body(gain_ref, bias_ref, out_ref):
    out_ref[0:4] = gain_ref[...].T
    out_ref[4:8] = bias_ref[...].T


WINDOW = 896


def window(z):
    return pl.ds(pl.multiple_of(768 * z, HD), WINDOW)


def window_body(s_ref, w_ref, out_ref):
    half = out_ref.shape[1]
    rows = pl.ds(pl.multiple_of(half * s_ref[2], 64), half)
    for i in range(4):
        out_ref[i] = w_ref[rows, 768 * i : 768 * i + WINDOW]


def out_body(s_ref, o0, o1, o2a, o2b, o3, mine, other, x_any, scale_ref, r_ref, stats_ref, w_ref, x_ref, sems):
    y, c, z = s_ref[0], s_ref[2], s_ref[3]
    half = mine.shape[1]
    upper = pl.ds(pl.multiple_of(half * c, 64), half)
    lower = pl.ds(pl.multiple_of(half * (1 - c), 64), half)
    copies = [
        pltpu.make_async_copy(mine, w_ref.at[:, upper], sems.at[0]),
        pltpu.make_async_copy(other, w_ref.at[:, lower], sems.at[1]),
        pltpu.make_async_copy(x_any.at[:, window(z)], x_ref, sems.at[2]),
    ]
    for copy in copies:
        copy.start()
    acc = jnp.zeros((ROWS, WINDOW), F32)
    for copy in copies:
        copy.wait()
    parts = [
        [o0[k] for k in range(4)],
        [o1[k] for k in range(4)],
        [o2a[0], o2a[1], o2b[0], o2b[1]],
        [o3[k] for k in range(4)],
    ]
    for j in range(4):
        heads = jnp.concatenate(parts[j], axis=1)
        plane = (z - j) & 3
        rows = jnp.concatenate(
            [w_ref[plane, pl.ds(pl.multiple_of(HD * ((y + k) & 3), HD), HD), :] for k in range(4)],
            axis=0,
        )
        acc = acc + cdot(heads, rows)
    residual = cdot(sub_row_permutation(), x_ref[...]) + scale_ref[:, window(z)] * acc
    residual = pltpu.roll(residual, WINDOW - 32 * z, 1)[:, 0 : r_ref.shape[2]]
    total = jnp.zeros((MROWS, 1), F32)
    squares = jnp.zeros((MROWS, 1), F32)
    for sub in range(4):
        part = residual[MROWS * sub : MROWS * (sub + 1)]
        r_ref[sub] = part
        total = total + jnp.sum(part, axis=1, keepdims=True)
        squares = squares + jnp.sum(part * part, axis=1, keepdims=True)
    lane = lax.broadcasted_iota(jnp.int32, (MROWS, HD), 1)
    stats_ref[...] = jnp.where(lane == 0, total, squares)


def interleave(parts):
    count = parts[0].shape[1]
    row = lax.broadcasted_iota(jnp.int32, (4 * count, 4 * count), 0)
    col = lax.broadcasted_iota(jnp.int32, (4 * count, 4 * count), 1)
    hit = row == (col & 3) * count + (col >> 2)
    return cdot(jnp.concatenate(parts, axis=1), jnp.where(hit, 1.0, 0.0).astype(BF)).astype(BF)


def merge_body(s0, s1, s2, s3, r_ref, affine_ref, out_ref):
    share = r_ref.shape[2]
    stats = ((s0[...] + s2[...]) + (s1[...] + s3[...])) * (1.0 / (16 * share))
    mean = stats[:, 0:1]
    scale = lax.rsqrt(stats[:, 1:2] - mean * mean + 1e-05)
    normed = []
    for sub in range(4):
        gain, bias = affine_ref[sub : sub + 1], affine_ref[4 + sub : 5 + sub]
        normed.append(((r_ref[sub] - mean) * scale * gain + bias).astype(BF))
    for start in range(0, share, HD):
        stop = min(start + HD, share)
        out_ref[:, 4 * start : 4 * stop] = interleave([n[:, start:stop] for n in normed])


def projection_body(s_ref, *refs):
    merged = refs[:10]
    weights = refs[10:17]
    outs = refs[17:21]
    a_ref, w_ref = refs[21:]
    y, x, c, z = s_ref[0], s_ref[1], s_ref[2], s_ref[3]
    for n, core in ((0, c), (5, 1 - c)):
        for part, (j, offset) in enumerate(((0, 0), (1, 0), (2, 0), (2, 48), (3, 0))):
            ref = merged[n + part]
            start = pl.multiple_of(ROWS * core + MROWS * ((x - j) & 3) + offset, 16)
            a_ref[pl.ds(start, ref.shape[0]), :] = ref[...]
    for ref, (j, offset) in zip(weights, ((0, 0), (1, 0), (1, 96), (2, 0), (2, 96), (3, 0), (3, 96))):
        start = pl.multiple_of(192 * ((y - j - z) & 3) + offset, 32)
        w_ref[pl.ds(start, ref.shape[0]), :] = ref[...]
    acc = lax.dot_general(
        a_ref[...], w_ref[...], (((1,), (1,)), ((), ())), preferred_element_type=F32
    )
    for n in range(4):
        block = acc[:, 192 * n : 192 * (n + 1)]
        packed = jnp.concatenate([block[0:ROWS], block[ROWS : 2 * ROWS]], axis=1)
        outs[n][...] = packed.astype(outs[n].dtype)


def place_body(s_ref, r0, r1, r2a, r2b, r3, slots_ref, text_ref, tslots_ref, own_ref, sib_ref, rows_ref):
    y, x, c = s_ref[0], s_ref[1], s_ref[2]

    def positions(core):
        row = lax.broadcasted_iota(jnp.int32, (448, 1), 0)
        k = (row >= 112).astype(jnp.int32) + (row >= 224).astype(jnp.int32) + (row >= 336).astype(jnp.int32)
        return 112 * (8 * y + 2 * ((x + k) & 3) + core) + row - 112 * k

    def pick(position, slots):
        return jnp.where(position == slots, 1.0, 0.0).astype(BF)

    for k, offset, r in ((0, 0, r0), (1, 0, r1), (2, 0, r2a), (2, 192, r2b), (3, 0, r3)):
        start = pl.multiple_of(ROWS * ((y - k) & 3) + offset, 64)
        both = r[...]
        rows_ref[pl.ds(start, r.shape[0]), :] = both[:, 0:192]
        rows_ref[pl.ds(4 * ROWS + start, r.shape[0]), :] = both[:, 192:384]
    rows, text = rows_ref[...], text_ref[...]
    for core, ref in ((1 - c, sib_ref), (c, own_ref)):
        where = positions(core)
        value = cdot(pick(where, slots_ref[...]), rows) + cdot(pick(where, tslots_ref[...]), text)
        ref[...] = value.astype(BF)


def stream_body(s_ref, b0, b1, b2, b3, out_ref, squares_ref):
    x, c = s_ref[1], s_ref[2]
    width = b0.shape[1]
    total = jnp.zeros((b0.shape[0], 1), F32)
    blocks = [b0[...], b1[...], b2[...], b3[...]]
    for place in range(4):
        k = (x - place) & 3
        value = blocks[0]
        for n in range(1, 4):
            value = jnp.where(k == n, blocks[n], value)
        turned = jnp.concatenate([value[:, 192:384], value[:, 0:192]], axis=1)
        value = jnp.where(c == 0, value, turned)
        out_ref[:, width * place : width * (place + 1)] = value
        wide = value.astype(F32)
        total = total + jnp.sum(wide * wide, axis=1, keepdims=True)
    squares_ref[...] = jnp.broadcast_to(total, squares_ref.shape)


def after(values):
    return lax.optimization_barrier(values)


def over_z(value):
    return [value] + [shift(value, "z", k) for k in (1, 2, 3)]


def ring(value, axis):
    half = value.shape[0] // 2
    back = shift(value, axis, 1)
    ahead = shift(value, axis, 3)
    return [value, back, shift(back[:half], axis, 1), shift(ahead[half:], axis, 3), ahead]


def per_device(
    patches,
    norm_gain,
    query_weight,
    key_weight,
    value_weight,
    out_weight,
    layer_scale,
    merge_gain,
    merge_bias,
    proj_weight,
    proj_bias,
    text_rows,
    stream_gain,
    tile_counts,
    image_slots,
    text_slots,
):
    y, x, c, z = [lax.axis_index(name).astype(jnp.int32) for name in ("y", "x", "c", "z")]
    coords = jnp.stack([y, x, c, z])
    width = patches.shape[1]
    share = width // 4

    kvq = project_qkv(coords, patches, norm_gain.reshape(width // HD, HD), key_weight, value_weight, query_weight)

    kvq, out_weight = after((kvq, out_weight))
    moved = [kvq[0]] + [shift(kvq[k], "y", k) for k in (1, 2, 3)]
    kv_own, q_own = call(
        pack_body,
        (
            jax.ShapeDtypeStruct((4, ROWS, 2 * HD), BF),
            jax.ShapeDtypeStruct((4, ROWS, HD), BF),
        ),
        1,
        in_specs=[VMEM] * 4,
    )(*moved)
    kv_own, q_own, proj_turned = after((kv_own, q_own, proj_weight.T))
    proj_low, proj_high = proj_turned[0:96], proj_turned[96:192]
    back_low, ahead_high = shift(proj_low, "y", 1), shift(proj_high, "y", 3)
    near = [shift(kv_own, "x", 1), shift(kv_own, "x", 3)]
    kv_sib = swap(kv_own)

    where = (coords, tile_counts, q_own)
    state = attend((0,) * 4, *where, [kv_own, kv_sib], None, False)
    out_weight, state = after((out_weight, state))
    windows = call(
        window_body,
        jax.ShapeDtypeStruct((4, out_weight.shape[0] // 2, WINDOW), BF),
        0.1,
        in_specs=[SMEM, VMEM],
    )(coords, out_weight)
    near, state, windows, back_low, ahead_high, proj_low, proj_high = after(
        (near, state, windows, back_low, ahead_high, proj_low, proj_high)
    )
    back_high, ahead_low = shift(proj_high, "y", 1), shift(proj_low, "y", 3)
    out_half = lax.all_to_all(windows, "z", 0, 0, tiled=True)
    far = [shift(near[0][0:2], "x", 1), shift(near[1][2:4], "x", 3)]
    blocks = [near[0], swap(near[0]), near[1], swap(near[1])]
    state = attend((1,) * 4 + (3,) * 4, *where, blocks, state, False)
    far, state, out_half, back_low, ahead_high, back_high, ahead_low = after(
        (far, state, out_half, back_low, ahead_high, back_high, ahead_low)
    )
    proj_parts = [
        proj_turned,
        back_low,
        back_high,
        shift(back_low, "y", 1),
        shift(ahead_high, "y", 3),
        ahead_low,
        ahead_high,
    ]
    blocks = [far[0], swap(far[0]), far[1], swap(far[1])]
    attended = attend((2,) * 4, *where, blocks, state, True)
    heads = jnp.stack([attended[0]] + [shift(attended[k], "y", 4 - k) for k in (1, 2, 3)])
    heads, merge_gain, merge_bias, layer_scale, text_rows, proj_bias, proj_parts = after(
        (heads, merge_gain, merge_bias, layer_scale, text_rows, proj_bias, proj_parts)
    )

    head_parts = ring(heads, "z")
    affine = call(
        turn_body, jax.ShapeDtypeStruct((8, share), F32), 1, in_specs=[VMEM] * 2
    )(merge_gain.reshape(share, 4), merge_bias.reshape(share, 4))
    turn = [(4 * a + b, 4 * b + a) for a in range(4) for b in range(4)]
    text = lax.ppermute(text_rows, ("y", "z"), turn)
    bias_row = lax.ppermute(proj_bias[None], ("y", "z"), turn)
    *head_parts, affine, swap_half, text, bias_row = after(
        (*head_parts, affine, swap(out_half), text, bias_row)
    )
    residual, stats = call(
        out_body,
        (
            jax.ShapeDtypeStruct((4, MROWS, share), F32),
            jax.ShapeDtypeStruct((MROWS, HD), F32),
        ),
        6,
        scratch=[
            pltpu.VMEM((4, 4 * HD, WINDOW), BF),
            pltpu.VMEM((ROWS, WINDOW), BF),
            pltpu.SemaphoreType.DMA((3,)),
        ],
        in_specs=[SMEM] + [VMEM] * 5 + [ANY] * 3 + [VMEM],
    )(coords, *head_parts, out_half, swap_half, patches, layer_scale[None])
    merged = call(
        merge_body, jax.ShapeDtypeStruct((MROWS, width), BF), 1, in_specs=[VMEM] * 6
    )(*over_z(stats), residual, affine)

    merged_parts = ring(merged, "x")
    merged, image_slots = after((merged, image_slots))
    slots = image_slots.reshape(16, 2, MROWS).transpose(1, 0, 2).reshape(1, 32 * MROWS)
    bias_row = jnp.concatenate([bias_row, bias_row], axis=1)
    merged_parts += [swap(part) for part in merged_parts]
    *merged_parts, slots, bias_row = after((*merged_parts, slots, bias_row))
    summed, *partial = call(
        projection_body,
        [jax.ShapeDtypeStruct((ROWS, ROWS), kind) for kind in (F32, BF, BF, BF)],
        8,
        scratch=[pltpu.VMEM((2 * ROWS, width), BF), pltpu.VMEM((2 * ROWS, width), BF)],
        in_specs=[SMEM] + [VMEM] * 17,
    )(coords, *merged_parts, *proj_parts)
    for k in (1, 2, 3):
        summed = summed + shift(partial[k - 1], "z", k).astype(F32)

    rows = jax.nn.gelu(summed + bias_row, approximate=False).astype(BF)

    row_parts = ring(rows, "y")
    placed, for_sibling = call(
        place_body,
        (
            jax.ShapeDtypeStruct((448, 192), BF),
            jax.ShapeDtypeStruct((448, 192), BF),
        ),
        4,
        scratch=[pltpu.VMEM((8 * ROWS, 192), BF)],
        in_specs=[SMEM] + [VMEM] * 8,
    )(coords, *row_parts, slots, text, text_slots[None])
    placed = jnp.concatenate([placed, swap(for_sibling)], axis=1).reshape(4, 112, ROWS)
    blocks = [placed[0]] + [shift(placed[k], "x", k) for k in (1, 2, 3)]
    stream, squares = call(
        stream_body,
        (
            jax.ShapeDtypeStruct((112, 4 * ROWS), BF),
            jax.ShapeDtypeStruct((112, HD), F32),
        ),
        2,
        in_specs=[SMEM] + [VMEM] * 4,
    )(coords, *blocks)
    squares = over_z(squares)
    squares = ((squares[0] + squares[2]) + (squares[1] + squares[3]))[:, 0:1]
    inverse_rms = lax.rsqrt(squares * (1.0 / 6144) + 1e-05)
    normed = (stream.astype(F32) * inverse_rms * stream_gain).astype(BF)
    return (stream, normed)


def solution(mesh):
    grid = Mesh(mesh.devices.reshape(4, 4, 2, 4), ("y", "x", "c", "z"))
    seq = ("y", "x", "c")
    return jax.shard_map(
        per_device,
        mesh=grid,
        in_specs=(
            P(seq, None),
            P(),
            P(None, "z"),
            P(None, "z"),
            P(None, "z"),
            P("z", None),
            P(),
            P("z"),
            P("z"),
            P("z", seq),
            P(seq),
            P(None, seq),
            P("z"),
            P(),
            P(),
            P(),
        ),
        out_specs=(P(seq, "z"), P(seq, "z")),
        check_vma=False,
    )
```

```python
import jax
import jax.numpy as jnp
from jax import lax
from jax.experimental import pallas as pl
from jax.experimental.pallas import tpu as pltpu
from jax.sharding import Mesh, PartitionSpec as P

HD = 128
ROWS = 384
MROWS = 96
BF = jnp.bfloat16
F32 = jnp.float32
LIMIT = 60 * 1024 * 1024


def cdot(a, b):
    return jnp.dot(a, b, preferred_element_type=F32)


def shift(value, axis, k):
    return lax.ppermute(value, axis, [(i, (i + k) % 4) for i in range(4)])


def swap(value):
    return lax.ppermute(value, "c", [(0, 1), (1, 0)])


def cost(us):
    return pl.CostEstimate(flops=int(us * 1.0e9), transcendentals=0, bytes_accessed=0)


def call(body, out_shape, us, scratch=(), **kw):
    return pl.pallas_call(
        body,
        out_shape=out_shape,
        scratch_shapes=scratch,
        cost_estimate=cost(us),
        compiler_params=pltpu.CompilerParams(vmem_limit_bytes=LIMIT),
        **kw,
    )


SMEM = pl.BlockSpec(memory_space=pltpu.SMEM)
VMEM = pl.BlockSpec(memory_space=pltpu.VMEM)
ANY = pl.BlockSpec(memory_space=pl.ANY)


def sub_row_permutation():
    row = lax.broadcasted_iota(jnp.int32, (ROWS, ROWS), 0)
    col = lax.broadcasted_iota(jnp.int32, (ROWS, ROWS), 1)
    sub = (row >= 96).astype(jnp.int32) + (row >= 192).astype(jnp.int32) + (row >= 288).astype(jnp.int32)
    m = row - 96 * sub
    source = (2 * (m >> 4) + (sub >> 1)) * 32 + 2 * (m & 15) + (sub & 1)
    return jnp.where(source == col, 1.0, 0.0).astype(BF)


def qkv_body(s_ref, x_ref, g_ref, wk_ref, wv_ref, wq_ref, o0, o1, o2, o3, xn_ref):
    half = pl.program_id(0)

    @pl.when(half == 0)
    def _():
        xf = cdot(sub_row_permutation(), x_ref[...])
        scale = lax.rsqrt(jnp.mean(xf * xf, axis=-1, keepdims=True) + 1e-06)
        gain = jnp.concatenate([g_ref[i : i + 1] for i in range(g_ref.shape[0])], axis=1)
        xn_ref[...] = (xf * scale * gain).astype(BF)

    xn = xn_ref[...]
    keys = cdot(xn, wk_ref[...]).astype(BF)
    values = cdot(xn, wv_ref[...]).astype(BF)
    queries = (cdot(xn, wq_ref[...]) * HD ** (-0.5)).astype(BF)
    for i in range(2):
        slot = (2 * half + i - s_ref[0]) & 3
        part = slice(HD * i, HD * (i + 1))
        head = jnp.concatenate([keys[:, part], values[:, part], queries[:, part]], axis=1)
        for k, ref in enumerate((o0, o1, o2, o3)):

            @pl.when(slot == k)
            def _(ref=ref, head=head):
                ref[...] = head


def project_qkv(y, patches, gain, wk, wv, wq):
    width = patches.shape[1]
    whole = pl.BlockSpec((ROWS, width), lambda j, s: (0, 0))
    weight = pl.BlockSpec((width, 2 * HD), lambda j, s: (0, j))
    return pl.pallas_call(
        qkv_body,
        out_shape=[jax.ShapeDtypeStruct((ROWS, 3 * HD), BF)] * 4,
        grid_spec=pltpu.PrefetchScalarGridSpec(
            num_scalar_prefetch=1,
            grid=(2,),
            in_specs=[whole, pl.BlockSpec((width // HD, HD), lambda j, s: (0, 0)), weight, weight, weight],
            out_specs=[pl.BlockSpec((ROWS, 3 * HD), lambda j, s: (0, 0))] * 4,
            scratch_shapes=[pltpu.VMEM((ROWS, width), BF)],
        ),
        cost_estimate=cost(11),
        compiler_params=pltpu.CompilerParams(
            dimension_semantics=("arbitrary",), vmem_limit_bytes=LIMIT
        ),
    )(y, patches, gain, wk, wv, wq)


def image_lanes(info, scale, same):
    row = lax.broadcasted_iota(jnp.int32, (ROWS, HD), 0)
    lane = lax.broadcasted_iota(jnp.int32, (ROWS, HD), 1)
    sub = (row >= 96).astype(jnp.int32) + (row >= 192).astype(jnp.int32) + (row >= 288).astype(jnp.int32)
    image = jnp.where((row - 96 * sub) * 4 < info[2], info[0], info[1])
    hit = lane == image if same else lane != image
    return jnp.where(hit, scale, 0.0).astype(BF)


def attention_body(steps, first, last, s_ref, t_ref, q_ref, *refs):
    rest = refs[:-3]
    own_ref, sib_ref, list_ref = refs[-3:]
    filled = 0
    while filled < len(steps):
        own, sib = rest[:2]
        rest = rest[2:]
        own_ref[filled : filled + own.shape[0]] = own[...]
        sib_ref[filled : filled + own.shape[0]] = sib[...]
        filled += own.shape[0]
    if not first:
        acc_in, max_in = rest[:2]
        rest = rest[2:]
    if last:
        *o_refs, acc_ref, max_ref = rest
    else:
        acc_ref, max_ref = rest
    if first:
        acc_ref[...] = jnp.zeros(acc_ref.shape, F32)
        max_ref[...] = jnp.full(max_ref.shape, -1e30, F32)
    else:
        acc_ref[...] = acc_in[...]
        max_ref[...] = max_in[...]
    y, x, c = s_ref[0], s_ref[1], s_ref[2]
    bound0 = 1024 * t_ref[0]
    bound1 = 1024 * (t_ref[0] + t_ref[1])

    def image_of(row):
        return (row >= bound0).astype(jnp.int32) + (row >= bound1).astype(jnp.int32)

    def block(yy, xx, cc):
        base = ROWS * (8 * yy + 2 * xx + cc)
        return image_of(base), image_of(base + ROWS - 1), 1024 - (base & 1023)

    def blocks_of(i):
        qb = i & 3
        kr = i >> 2
        step = steps[0] if len(steps) == 4 else jnp.where(kr < 4, steps[0], steps[4])
        xk = (x - step) & 3
        ki = [block((y - kr) & 3, xk, cc) for cc in (c, 1 - c)]
        return qb, kr, block((y - qb) & 3, x, c), ki

    def note(i, count):
        qb, kr, qi, ki = blocks_of(i)
        low = jnp.minimum(ki[0][0], ki[1][0])
        high = jnp.maximum(ki[0][1], ki[1][1])
        meets = jnp.logical_and(qi[1] >= low, qi[0] <= high)
        list_ref[count] = i
        return count + meets.astype(jnp.int32)

    def score(i, live):
        qb, kr, qi, ki = blocks_of(i)
        qi = (jnp.where(live, qi[0], 99), jnp.where(live, qi[1], 99), qi[2])
        q = jnp.concatenate([q_ref[qb], image_lanes(qi, -1e30, False)], axis=1)
        keys, values = [], []
        for n, ref in enumerate((own_ref, sib_ref)):
            keys.append(jnp.concatenate([ref[kr, :, 0:HD], image_lanes(ki[n], 1.0, True)], axis=1))
            values.append(
                jnp.concatenate([ref[kr, :, HD : 2 * HD], jnp.ones((ROWS, HD), BF)], axis=1)
            )
        scores = lax.dot_general(
            q, jnp.concatenate(keys, axis=0), (((1,), (1,)), ((), ())), preferred_element_type=F32
        )
        return qb, scores, jnp.concatenate(values, axis=0)

    def fold(qb, scores, values):
        old = max_ref[qb]
        new = jnp.maximum(old, jnp.max(scores, axis=1, keepdims=True))
        factor = jnp.exp(old - new)
        weights = jnp.exp(scores - new[:, 0:1]).astype(BF)
        max_ref[qb] = new
        acc_ref[qb] = acc_ref[qb] * jnp.concatenate([factor, factor], axis=1) + cdot(weights, values)

    def alone(t, carry):
        fold(*score(list_ref[t], True))
        return carry

    def two(t, carry):
        odd = 2 * t + 1 < count
        one = score(list_ref[2 * t], True)
        other = score(list_ref[jnp.where(odd, 2 * t + 1, 2 * t)], odd)
        fold(*one)
        fold(*other)
        return carry

    count = lax.fori_loop(0, 4 * len(steps), note, jnp.int32(0))
    if first:
        lax.fori_loop(0, count, alone, 0)
    else:
        lax.fori_loop(0, (count + 1) >> 1, two, 0)
    if last:
        for b in range(4):
            o_refs[b][...] = (acc_ref[b, :, 0:HD] / acc_ref[b, :, HD : 2 * HD]).astype(BF)


def attend(steps, coords, tile_counts, q, blocks, state, last):
    first = state is None
    state_shapes = [
        jax.ShapeDtypeStruct((4, ROWS, 2 * HD), F32),
        jax.ShapeDtypeStruct((4, ROWS, HD), F32),
    ]
    args = [coords, tile_counts, q, *blocks] + ([] if first else list(state))

    def body(*refs):
        attention_body(steps, first, last, *refs)

    specs = [SMEM, SMEM] + [VMEM] * (len(args) - 2)
    held = [pltpu.VMEM((len(steps), ROWS, 2 * HD), BF)] * 2 + [pltpu.SMEM((64,), jnp.int32)]
    if last:
        return call(
            body,
            [jax.ShapeDtypeStruct((ROWS, HD), BF)] * 4,
            2.5 * len(steps),
            scratch=[pltpu.VMEM(s.shape, s.dtype) for s in state_shapes] + held,
            in_specs=specs,
        )(*args)
    return call(body, state_shapes, 2.5 * len(steps), scratch=held, in_specs=specs)(*args)


def pack_body(m0, m1, m2, m3, kv_ref, q_ref):
    for k, ref in enumerate((m0, m1, m2, m3)):
        kv_ref[k] = ref[:, 0 : 2 * HD]
        q_ref[k] = ref[:, 2 * HD : 3 * HD]


def turn_body(gain_ref, bias_ref, out_ref):
    out_ref[0:4] = gain_ref[...].T
    out_ref[4:8] = bias_ref[...].T


WINDOW = 896


def window(z):
    return pl.ds(pl.multiple_of(768 * z, HD), WINDOW)


def window_body(s_ref, w_ref, out_ref):
    half = out_ref.shape[1]
    rows = pl.ds(pl.multiple_of(half * s_ref[2], 64), half)
    for i in range(4):
        out_ref[i] = w_ref[rows, 768 * i : 768 * i + WINDOW]


def out_body(s_ref, o0, o1, o2, o3, mine, other, x_any, scale_ref, r_ref, stats_ref, w_ref, x_ref, sems):
    y, c, z = s_ref[0], s_ref[2], s_ref[3]
    half = mine.shape[1]
    upper = pl.ds(pl.multiple_of(half * c, 64), half)
    lower = pl.ds(pl.multiple_of(half * (1 - c), 64), half)
    copies = [
        pltpu.make_async_copy(mine, w_ref.at[:, upper], sems.at[0]),
        pltpu.make_async_copy(other, w_ref.at[:, lower], sems.at[1]),
        pltpu.make_async_copy(x_any.at[:, window(z)], x_ref, sems.at[2]),
    ]
    for copy in copies:
        copy.start()
    acc = jnp.zeros((ROWS, WINDOW), F32)
    for copy in copies:
        copy.wait()
    parts = [
        [o0[k] for k in range(4)],
        [o1[k] for k in range(4)],
        [o2[k] for k in range(4)],
        [o3[k] for k in range(4)],
    ]
    for j in range(4):
        heads = jnp.concatenate(parts[j], axis=1)
        plane = (z - j) & 3
        rows = jnp.concatenate(
            [w_ref[plane, pl.ds(pl.multiple_of(HD * ((y + k) & 3), HD), HD), :] for k in range(4)],
            axis=0,
        )
        acc = acc + cdot(heads, rows)
    residual = cdot(sub_row_permutation(), x_ref[...]) + scale_ref[:, window(z)] * acc
    residual = pltpu.roll(residual, WINDOW - 32 * z, 1)[:, 0 : r_ref.shape[2]]
    total = jnp.zeros((MROWS, 1), F32)
    squares = jnp.zeros((MROWS, 1), F32)
    for sub in range(4):
        part = residual[MROWS * sub : MROWS * (sub + 1)]
        r_ref[sub] = part
        total = total + jnp.sum(part, axis=1, keepdims=True)
        squares = squares + jnp.sum(part * part, axis=1, keepdims=True)
    lane = lax.broadcasted_iota(jnp.int32, (MROWS, HD), 1)
    stats_ref[...] = jnp.where(lane == 0, total, squares)


def interleave(parts):
    count = parts[0].shape[1]
    row = lax.broadcasted_iota(jnp.int32, (4 * count, 4 * count), 0)
    col = lax.broadcasted_iota(jnp.int32, (4 * count, 4 * count), 1)
    hit = row == (col & 3) * count + (col >> 2)
    return cdot(jnp.concatenate(parts, axis=1), jnp.where(hit, 1.0, 0.0).astype(BF)).astype(BF)


def merge_body(s0, s1, s2, s3, r_ref, affine_ref, out_ref):
    share = r_ref.shape[2]
    stats = ((s0[...] + s2[...]) + (s1[...] + s3[...])) * (1.0 / (16 * share))
    mean = stats[:, 0:1]
    scale = lax.rsqrt(stats[:, 1:2] - mean * mean + 1e-05)
    normed = []
    for sub in range(4):
        gain, bias = affine_ref[sub : sub + 1], affine_ref[4 + sub : 5 + sub]
        normed.append(((r_ref[sub] - mean) * scale * gain + bias).astype(BF))
    for start in range(0, share, HD):
        stop = min(start + HD, share)
        out_ref[:, 4 * start : 4 * stop] = interleave([n[:, start:stop] for n in normed])


def projection_body(s_ref, *refs):
    merged = refs[:10]
    weights = refs[10:17]
    outs = refs[17:21]
    a_ref, w_ref = refs[21:]
    y, x, c, z = s_ref[0], s_ref[1], s_ref[2], s_ref[3]
    for n, core in ((0, c), (5, 1 - c)):
        for part, (j, offset) in enumerate(((0, 0), (1, 0), (2, 0), (2, 48), (3, 0))):
            ref = merged[n + part]
            start = pl.multiple_of(ROWS * core + MROWS * ((x - j) & 3) + offset, 16)
            a_ref[pl.ds(start, ref.shape[0]), :] = ref[...]
    for ref, (j, offset) in zip(weights, ((0, 0), (1, 0), (1, 96), (2, 0), (2, 96), (3, 0), (3, 96))):
        start = pl.multiple_of(192 * ((y - j - z) & 3) + offset, 32)
        w_ref[pl.ds(start, ref.shape[0]), :] = ref[...]

    def rows_block(i, carry):
        rows = pl.ds(pl.multiple_of(192 * i, 64), 192)
        lower = pl.ds(pl.multiple_of(192 * i + ROWS, 64), 192)
        values = jnp.concatenate([a_ref[rows, :], a_ref[lower, :]], axis=0)
        acc = lax.dot_general(
            values, w_ref[...], (((1,), (1,)), ((), ())), preferred_element_type=F32
        )
        for n in range(4):
            block = acc[:, 192 * n : 192 * (n + 1)]
            packed = jnp.concatenate([block[0:192], block[192:ROWS]], axis=1)
            outs[n][rows, :] = packed.astype(outs[n].dtype)
        return carry

    lax.fori_loop(0, 2, rows_block, 0)


def place_body(s_ref, r0, r1, r2, r3, slots_ref, text_ref, tslots_ref, own_ref, sib_ref, rows_ref, both_ref):
    y, x, c = s_ref[0], s_ref[1], s_ref[2]

    def positions(core):
        row = lax.broadcasted_iota(jnp.int32, (448, 1), 0)
        k = (row >= 112).astype(jnp.int32) + (row >= 224).astype(jnp.int32) + (row >= 336).astype(jnp.int32)
        return 112 * (8 * y + 2 * ((x + k) & 3) + core) + row - 112 * k

    def pick(position, slots):
        return jnp.where(position == slots, 1.0, 0.0).astype(BF)

    for k, r in enumerate((r0, r1, r2, r3)):
        start = pl.multiple_of(ROWS * ((y - k) & 3), ROWS)
        both = r[...]
        rows_ref[pl.ds(start, r.shape[0]), :] = both[:, 0:192]
        rows_ref[pl.ds(4 * ROWS + start, r.shape[0]), :] = both[:, 192:384]

    def core_block(n, carry):
        where = positions(jnp.where(n == 0, c, 1 - c))
        value = cdot(pick(where, slots_ref[...]), rows_ref[...])
        value = value + cdot(pick(where, tslots_ref[...]), text_ref[...])
        both_ref[n] = value.astype(BF)
        return carry

    lax.fori_loop(0, 2, core_block, 0)
    own_ref[...] = both_ref[0]
    sib_ref[...] = both_ref[1]


def stream_body(s_ref, b0, b1, b2, b3, out_ref, squares_ref):
    x, c = s_ref[1], s_ref[2]
    width = b0.shape[1]
    total = jnp.zeros((b0.shape[0], 1), F32)
    blocks = [b0[...], b1[...], b2[...], b3[...]]
    for place in range(4):
        k = (x - place) & 3
        value = blocks[0]
        for n in range(1, 4):
            value = jnp.where(k == n, blocks[n], value)
        turned = jnp.concatenate([value[:, 192:384], value[:, 0:192]], axis=1)
        value = jnp.where(c == 0, value, turned)
        out_ref[:, width * place : width * (place + 1)] = value
        wide = value.astype(F32)
        total = total + jnp.sum(wide * wide, axis=1, keepdims=True)
    squares_ref[...] = jnp.broadcast_to(total, squares_ref.shape)


def after(values):
    return lax.optimization_barrier(values)


def over_z(value):
    return [value] + [shift(value, "z", k) for k in (1, 2, 3)]


def ring(value, axis):
    half = value.shape[0] // 2
    back = shift(value, axis, 1)
    ahead = shift(value, axis, 3)
    return [value, back, shift(back[:half], axis, 1), shift(ahead[half:], axis, 3), ahead]


def per_device(
    patches,
    norm_gain,
    query_weight,
    key_weight,
    value_weight,
    out_weight,
    layer_scale,
    merge_gain,
    merge_bias,
    proj_weight,
    proj_bias,
    text_rows,
    stream_gain,
    tile_counts,
    image_slots,
    text_slots,
):
    y, x, c, z = [lax.axis_index(name).astype(jnp.int32) for name in ("y", "x", "c", "z")]
    coords = jnp.stack([y, x, c, z])
    width = patches.shape[1]
    share = width // 4

    kvq = project_qkv(coords, patches, norm_gain.reshape(width // HD, HD), key_weight, value_weight, query_weight)

    kvq, out_weight = after((kvq, out_weight))
    moved = [kvq[0]] + [shift(kvq[k], "y", k) for k in (1, 2, 3)]
    kv_own, q_own = call(
        pack_body,
        (
            jax.ShapeDtypeStruct((4, ROWS, 2 * HD), BF),
            jax.ShapeDtypeStruct((4, ROWS, HD), BF),
        ),
        1,
        in_specs=[VMEM] * 4,
    )(*moved)
    kv_own, q_own, proj_turned = after((kv_own, q_own, proj_weight.T))
    proj_low, proj_high = proj_turned[0:96], proj_turned[96:192]
    back_low, ahead_high = shift(proj_low, "y", 1), shift(proj_high, "y", 3)
    near = [shift(kv_own, "x", 1), shift(kv_own, "x", 3)]
    kv_sib = swap(kv_own)

    where = (coords, tile_counts, q_own)
    state = attend((0,) * 4, *where, [kv_own, kv_sib], None, False)
    out_weight, state = after((out_weight, state))
    windows = call(
        window_body,
        jax.ShapeDtypeStruct((4, out_weight.shape[0] // 2, WINDOW), BF),
        0.1,
        in_specs=[SMEM, VMEM],
    )(coords, out_weight)
    near, state, windows, back_low, ahead_high, proj_low, proj_high, kv_here = after(
        (near, state, windows, back_low, ahead_high, proj_low, proj_high, kv_own)
    )
    back_high, ahead_low = shift(proj_high, "y", 1), shift(proj_low, "y", 3)
    out_half = lax.all_to_all(windows, "z", 0, 0, tiled=True)
    far = shift(kv_here, "x", 2)
    blocks = [near[0], swap(near[0]), near[1], swap(near[1])]
    state = attend((1,) * 4 + (3,) * 4, *where, blocks, state, False)
    far, state, out_half, back_low, ahead_high, back_high, ahead_low = after(
        (far, state, out_half, back_low, ahead_high, back_high, ahead_low)
    )
    proj_parts = [
        proj_turned,
        back_low,
        back_high,
        shift(back_low, "y", 1),
        shift(ahead_high, "y", 3),
        ahead_low,
        ahead_high,
    ]
    attended = attend((2,) * 4, *where, [far, swap(far)], state, True)
    heads = jnp.stack([attended[0]] + [shift(attended[k], "y", 4 - k) for k in (1, 2, 3)])
    heads, merge_gain, merge_bias, layer_scale, text_rows, proj_bias, proj_parts, out_half = after(
        (heads, merge_gain, merge_bias, layer_scale, text_rows, proj_bias, proj_parts, out_half)
    )

    head_parts = [heads] + [shift(heads, "z", k) for k in (1, 2, 3)]
    affine = call(
        turn_body, jax.ShapeDtypeStruct((8, share), F32), 1, in_specs=[VMEM] * 2
    )(merge_gain.reshape(share, 4), merge_bias.reshape(share, 4))
    turn = [(4 * a + b, 4 * b + a) for a in range(4) for b in range(4)]
    text = lax.ppermute(text_rows, ("y", "z"), turn)
    bias_row = lax.ppermute(proj_bias[None], ("y", "z"), turn)
    *head_parts, affine, swap_half, text, bias_row = after(
        (*head_parts, affine, swap(out_half), text, bias_row)
    )
    residual, stats = call(
        out_body,
        (
            jax.ShapeDtypeStruct((4, MROWS, share), F32),
            jax.ShapeDtypeStruct((MROWS, HD), F32),
        ),
        6,
        scratch=[
            pltpu.VMEM((4, 4 * HD, WINDOW), BF),
            pltpu.VMEM((ROWS, WINDOW), BF),
            pltpu.SemaphoreType.DMA((3,)),
        ],
        in_specs=[SMEM] + [VMEM] * 4 + [ANY] * 3 + [VMEM],
    )(coords, *head_parts, out_half, swap_half, patches, layer_scale[None])
    merged = call(
        merge_body, jax.ShapeDtypeStruct((MROWS, width), BF), 1, in_specs=[VMEM] * 6
    )(*over_z(stats), residual, affine)

    merged_parts = ring(merged, "x")
    merged, image_slots = after((merged, image_slots))
    slots = image_slots.reshape(16, 2, MROWS).transpose(1, 0, 2).reshape(1, 32 * MROWS)
    bias_row = jnp.concatenate([bias_row, bias_row], axis=1)
    merged_parts += [swap(part) for part in merged_parts]
    *merged_parts, slots, bias_row = after((*merged_parts, slots, bias_row))
    summed, *partial = call(
        projection_body,
        [jax.ShapeDtypeStruct((ROWS, ROWS), kind) for kind in (F32, BF, BF, BF)],
        8,
        scratch=[pltpu.VMEM((2 * ROWS, width), BF), pltpu.VMEM((2 * ROWS, width), BF)],
        in_specs=[SMEM] + [VMEM] * 17,
    )(coords, *merged_parts, *proj_parts)
    for k in (1, 2, 3):
        summed = summed + shift(partial[k - 1], "z", k).astype(F32)

    rows = jax.nn.gelu(summed + bias_row, approximate=False).astype(BF)

    row_parts = [rows] + [shift(rows, "y", k) for k in (1, 2, 3)]
    placed, for_sibling = call(
        place_body,
        (
            jax.ShapeDtypeStruct((448, 192), BF),
            jax.ShapeDtypeStruct((448, 192), BF),
        ),
        4,
        scratch=[pltpu.VMEM((8 * ROWS, 192), BF), pltpu.VMEM((2, 448, 192), BF)],
        in_specs=[SMEM] + [VMEM] * 7,
    )(coords, *row_parts, slots, text, text_slots[None])
    placed = jnp.concatenate([placed, swap(for_sibling)], axis=1).reshape(4, 112, ROWS)
    blocks = [placed[0]] + [shift(placed[k], "x", k) for k in (1, 2, 3)]
    stream, squares = call(
        stream_body,
        (
            jax.ShapeDtypeStruct((112, 4 * ROWS), BF),
            jax.ShapeDtypeStruct((112, HD), F32),
        ),
        2,
        in_specs=[SMEM] + [VMEM] * 4,
    )(coords, *blocks)
    squares = over_z(squares)
    squares = ((squares[0] + squares[2]) + (squares[1] + squares[3]))[:, 0:1]
    inverse_rms = lax.rsqrt(squares * (1.0 / 6144) + 1e-05)
    normed = (stream.astype(F32) * inverse_rms * stream_gain).astype(BF)
    return (stream, normed)


def solution(mesh):
    grid = Mesh(mesh.devices.reshape(4, 4, 2, 4), ("y", "x", "c", "z"))
    seq = ("y", "x", "c")
    return jax.shard_map(
        per_device,
        mesh=grid,
        in_specs=(
            P(seq, None),
            P(),
            P(None, "z"),
            P(None, "z"),
            P(None, "z"),
            P("z", None),
            P(),
            P("z"),
            P("z"),
            P("z", seq),
            P(seq),
            P(None, seq),
            P("z"),
            P(),
            P(),
            P(),
        ),
        out_specs=(P(seq, "z"), P(seq, "z")),
        check_vma=False,
    )
```

```python
import jax
import jax.numpy as jnp
from jax import lax
from jax.experimental import pallas as pl
from jax.experimental.pallas import tpu as pltpu
from jax.sharding import Mesh, PartitionSpec as P

HD = 128
ROWS = 384
MROWS = 96
BF = jnp.bfloat16
F32 = jnp.float32
LIMIT = 60 * 1024 * 1024


def cdot(a, b):
    return jnp.dot(a, b, preferred_element_type=F32)


def shift(value, axis, k):
    return lax.ppermute(value, axis, [(i, (i + k) % 4) for i in range(4)])


def swap(value):
    return lax.ppermute(value, "c", [(0, 1), (1, 0)])


def cost(us):
    return pl.CostEstimate(flops=int(us * 1.0e9), transcendentals=0, bytes_accessed=0)


def call(body, out_shape, us, scratch=(), **kw):
    return pl.pallas_call(
        body,
        out_shape=out_shape,
        scratch_shapes=scratch,
        cost_estimate=cost(us),
        compiler_params=pltpu.CompilerParams(vmem_limit_bytes=LIMIT),
        **kw,
    )


SMEM = pl.BlockSpec(memory_space=pltpu.SMEM)
VMEM = pl.BlockSpec(memory_space=pltpu.VMEM)
ANY = pl.BlockSpec(memory_space=pl.ANY)


def sub_row_permutation():
    row = lax.broadcasted_iota(jnp.int32, (ROWS, ROWS), 0)
    col = lax.broadcasted_iota(jnp.int32, (ROWS, ROWS), 1)
    sub = (row >= 96).astype(jnp.int32) + (row >= 192).astype(jnp.int32) + (row >= 288).astype(jnp.int32)
    m = row - 96 * sub
    source = (2 * (m >> 4) + (sub >> 1)) * 32 + 2 * (m & 15) + (sub & 1)
    return jnp.where(source == col, 1.0, 0.0).astype(BF)


def qkv_body(s_ref, x_ref, g_ref, wk_ref, wv_ref, wq_ref, o0, o1, o2, o3, xn_ref):
    half = pl.program_id(0)

    @pl.when(half == 0)
    def _():
        xf = cdot(sub_row_permutation(), x_ref[...])
        scale = lax.rsqrt(jnp.mean(xf * xf, axis=-1, keepdims=True) + 1e-06)
        gain = jnp.concatenate([g_ref[i : i + 1] for i in range(g_ref.shape[0])], axis=1)
        xn_ref[...] = (xf * scale * gain).astype(BF)

    xn = xn_ref[...]
    keys = cdot(xn, wk_ref[...]).astype(BF)
    values = cdot(xn, wv_ref[...]).astype(BF)
    queries = (cdot(xn, wq_ref[...]) * HD ** (-0.5)).astype(BF)
    for i in range(2):
        slot = (2 * half + i - s_ref[0]) & 3
        part = slice(HD * i, HD * (i + 1))
        head = jnp.concatenate([keys[:, part], values[:, part], queries[:, part]], axis=1)
        for k, ref in enumerate((o0, o1, o2, o3)):

            @pl.when(slot == k)
            def _(ref=ref, head=head):
                ref[...] = head


def project_qkv(y, patches, gain, wk, wv, wq):
    width = patches.shape[1]
    whole = pl.BlockSpec((ROWS, width), lambda j, s: (0, 0))
    weight = pl.BlockSpec((width, 2 * HD), lambda j, s: (0, j))
    return pl.pallas_call(
        qkv_body,
        out_shape=[jax.ShapeDtypeStruct((ROWS, 3 * HD), BF)] * 4,
        grid_spec=pltpu.PrefetchScalarGridSpec(
            num_scalar_prefetch=1,
            grid=(2,),
            in_specs=[whole, pl.BlockSpec((width // HD, HD), lambda j, s: (0, 0)), weight, weight, weight],
            out_specs=[pl.BlockSpec((ROWS, 3 * HD), lambda j, s: (0, 0))] * 4,
            scratch_shapes=[pltpu.VMEM((ROWS, width), BF)],
        ),
        cost_estimate=cost(11),
        compiler_params=pltpu.CompilerParams(
            dimension_semantics=("arbitrary",), vmem_limit_bytes=LIMIT
        ),
    )(y, patches, gain, wk, wv, wq)


def image_lanes(info, scale, same):
    row = lax.broadcasted_iota(jnp.int32, (ROWS, HD), 0)
    lane = lax.broadcasted_iota(jnp.int32, (ROWS, HD), 1)
    sub = (row >= 96).astype(jnp.int32) + (row >= 192).astype(jnp.int32) + (row >= 288).astype(jnp.int32)
    image = jnp.where((row - 96 * sub) * 4 < info[2], info[0], info[1])
    hit = lane == image if same else lane != image
    return jnp.where(hit, scale, 0.0).astype(BF)


def attention_body(steps, first, last, s_ref, t_ref, q_ref, *refs):
    rest = refs[:-3]
    own_ref, sib_ref, list_ref = refs[-3:]
    filled = 0
    while filled < len(steps):
        own, sib = rest[:2]
        rest = rest[2:]
        own_ref[filled : filled + own.shape[0]] = own[...]
        sib_ref[filled : filled + own.shape[0]] = sib[...]
        filled += own.shape[0]
    if not first:
        acc_in, max_in = rest[:2]
        rest = rest[2:]
    if last:
        *o_refs, acc_ref, max_ref = rest
    else:
        acc_ref, max_ref = rest
    if first:
        acc_ref[...] = jnp.zeros(acc_ref.shape, F32)
        max_ref[...] = jnp.full(max_ref.shape, -1e30, F32)
    else:
        acc_ref[...] = acc_in[...]
        max_ref[...] = max_in[...]
    y, x, c = s_ref[0], s_ref[1], s_ref[2]
    bound0 = 1024 * t_ref[0]
    bound1 = 1024 * (t_ref[0] + t_ref[1])

    def image_of(row):
        return (row >= bound0).astype(jnp.int32) + (row >= bound1).astype(jnp.int32)

    def block(yy, xx, cc):
        base = ROWS * (8 * yy + 2 * xx + cc)
        return image_of(base), image_of(base + ROWS - 1), 1024 - (base & 1023)

    def blocks_of(i):
        qb = i & 3
        kr = i >> 2
        step = steps[0] if len(steps) == 4 else jnp.where(kr < 4, steps[0], steps[4])
        xk = (x - step) & 3
        ki = [block((y - kr) & 3, xk, cc) for cc in (c, 1 - c)]
        return qb, kr, block((y - qb) & 3, x, c), ki

    def note(i, count):
        qb, kr, qi, ki = blocks_of(i)
        low = jnp.minimum(ki[0][0], ki[1][0])
        high = jnp.maximum(ki[0][1], ki[1][1])
        meets = jnp.logical_and(qi[1] >= low, qi[0] <= high)
        list_ref[count] = i
        return count + meets.astype(jnp.int32)

    def score(i, live):
        qb, kr, qi, ki = blocks_of(i)
        qi = (jnp.where(live, qi[0], 99), jnp.where(live, qi[1], 99), qi[2])
        q = jnp.concatenate([q_ref[qb], image_lanes(qi, -1e30, False)], axis=1)
        keys, values = [], []
        for n, ref in enumerate((own_ref, sib_ref)):
            keys.append(jnp.concatenate([ref[kr, :, 0:HD], image_lanes(ki[n], 1.0, True)], axis=1))
            values.append(
                jnp.concatenate([ref[kr, :, HD : 2 * HD], jnp.ones((ROWS, HD), BF)], axis=1)
            )
        scores = lax.dot_general(
            q, jnp.concatenate(keys, axis=0), (((1,), (1,)), ((), ())), preferred_element_type=F32
        )
        return qb, scores, jnp.concatenate(values, axis=0)

    def fold(qb, scores, values):
        old = max_ref[qb]
        new = jnp.maximum(old, jnp.max(scores, axis=1, keepdims=True))
        factor = jnp.exp(old - new)
        weights = jnp.exp(scores - new[:, 0:1]).astype(BF)
        max_ref[qb] = new
        acc_ref[qb] = acc_ref[qb] * jnp.concatenate([factor, factor], axis=1) + cdot(weights, values)

    def alone(t, carry):
        fold(*score(list_ref[t], True))
        return carry

    def two(t, carry):
        odd = 2 * t + 1 < count
        one = score(list_ref[2 * t], True)
        other = score(list_ref[jnp.where(odd, 2 * t + 1, 2 * t)], odd)
        fold(*one)
        fold(*other)
        return carry

    count = lax.fori_loop(0, 4 * len(steps), note, jnp.int32(0))
    if first:
        lax.fori_loop(0, count, alone, 0)
    else:
        lax.fori_loop(0, (count + 1) >> 1, two, 0)
    if last:
        for b in range(4):
            o_refs[b][...] = (acc_ref[b, :, 0:HD] / acc_ref[b, :, HD : 2 * HD]).astype(BF)


def attend(steps, coords, tile_counts, q, blocks, state, last):
    first = state is None
    state_shapes = [
        jax.ShapeDtypeStruct((4, ROWS, 2 * HD), F32),
        jax.ShapeDtypeStruct((4, ROWS, HD), F32),
    ]
    args = [coords, tile_counts, q, *blocks] + ([] if first else list(state))

    def body(*refs):
        attention_body(steps, first, last, *refs)

    specs = [SMEM, SMEM] + [VMEM] * (len(args) - 2)
    held = [pltpu.VMEM((len(steps), ROWS, 2 * HD), BF)] * 2 + [pltpu.SMEM((64,), jnp.int32)]
    if last:
        return call(
            body,
            [jax.ShapeDtypeStruct((ROWS, HD), BF)] * 4,
            2.5 * len(steps),
            scratch=[pltpu.VMEM(s.shape, s.dtype) for s in state_shapes] + held,
            in_specs=specs,
        )(*args)
    return call(body, state_shapes, 2.5 * len(steps), scratch=held, in_specs=specs)(*args)


def pack_body(m0, m1, m2, m3, kv_ref, q_ref):
    for k, ref in enumerate((m0, m1, m2, m3)):
        kv_ref[k] = ref[:, 0 : 2 * HD]
        q_ref[k] = ref[:, 2 * HD : 3 * HD]


def turn_body(gain_ref, bias_ref, out_ref):
    out_ref[0:4] = gain_ref[...].T
    out_ref[4:8] = bias_ref[...].T


WINDOW = 896


def window(z):
    return pl.ds(pl.multiple_of(768 * z, HD), WINDOW)


def window_body(s_ref, w_ref, out_ref):
    half = out_ref.shape[1]
    rows = pl.ds(pl.multiple_of(half * s_ref[2], 64), half)
    for i in range(4):
        out_ref[i] = w_ref[rows, 768 * i : 768 * i + WINDOW]


def out_body(s_ref, o0, o1, o2, o3, mine, other, x_any, scale_ref, r_ref, stats_ref, w_ref, x_ref, sems):
    y, c, z = s_ref[0], s_ref[2], s_ref[3]
    half = mine.shape[1]
    upper = pl.ds(pl.multiple_of(half * c, 64), half)
    lower = pl.ds(pl.multiple_of(half * (1 - c), 64), half)
    copies = [
        pltpu.make_async_copy(mine, w_ref.at[:, upper], sems.at[0]),
        pltpu.make_async_copy(other, w_ref.at[:, lower], sems.at[1]),
        pltpu.make_async_copy(x_any.at[:, window(z)], x_ref, sems.at[2]),
    ]
    for copy in copies:
        copy.start()
    acc = jnp.zeros((ROWS, WINDOW), F32)
    for copy in copies:
        copy.wait()
    parts = [
        [o0[k] for k in range(4)],
        [o1[k] for k in range(4)],
        [o2[k] for k in range(4)],
        [o3[k] for k in range(4)],
    ]
    for j in range(4):
        heads = jnp.concatenate(parts[j], axis=1)
        plane = (z - j) & 3
        rows = jnp.concatenate(
            [w_ref[plane, pl.ds(pl.multiple_of(HD * ((y + k) & 3), HD), HD), :] for k in range(4)],
            axis=0,
        )
        acc = acc + cdot(heads, rows)
    residual = cdot(sub_row_permutation(), x_ref[...]) + scale_ref[:, window(z)] * acc
    residual = pltpu.roll(residual, WINDOW - 32 * z, 1)[:, 0 : r_ref.shape[2]]
    total = jnp.zeros((MROWS, 1), F32)
    squares = jnp.zeros((MROWS, 1), F32)
    for sub in range(4):
        part = residual[MROWS * sub : MROWS * (sub + 1)]
        r_ref[sub] = part
        total = total + jnp.sum(part, axis=1, keepdims=True)
        squares = squares + jnp.sum(part * part, axis=1, keepdims=True)
    lane = lax.broadcasted_iota(jnp.int32, (MROWS, HD), 1)
    stats_ref[...] = jnp.where(lane == 0, total, squares)


def interleave(parts):
    count = parts[0].shape[1]
    row = lax.broadcasted_iota(jnp.int32, (4 * count, 4 * count), 0)
    col = lax.broadcasted_iota(jnp.int32, (4 * count, 4 * count), 1)
    hit = row == (col & 3) * count + (col >> 2)
    return cdot(jnp.concatenate(parts, axis=1), jnp.where(hit, 1.0, 0.0).astype(BF)).astype(BF)


def merge_body(s0, s1, s2, s3, r_ref, affine_ref, out_ref):
    share = r_ref.shape[2]
    stats = ((s0[...] + s2[...]) + (s1[...] + s3[...])) * (1.0 / (16 * share))
    mean = stats[:, 0:1]
    scale = lax.rsqrt(stats[:, 1:2] - mean * mean + 1e-05)
    normed = []
    for sub in range(4):
        gain, bias = affine_ref[sub : sub + 1], affine_ref[4 + sub : 5 + sub]
        normed.append(((r_ref[sub] - mean) * scale * gain + bias).astype(BF))
    for start in range(0, share, HD):
        stop = min(start + HD, share)
        out_ref[:, 4 * start : 4 * stop] = interleave([n[:, start:stop] for n in normed])


def projection_body(s_ref, *refs):
    merged = refs[:10]
    weights = refs[10:17]
    outs = refs[17:21]
    a_ref, w_ref = refs[21:]
    y, x, c, z = s_ref[0], s_ref[1], s_ref[2], s_ref[3]
    for n, core in ((0, c), (5, 1 - c)):
        for part, (j, offset) in enumerate(((0, 0), (1, 0), (2, 0), (2, 48), (3, 0))):
            ref = merged[n + part]
            start = pl.multiple_of(ROWS * core + MROWS * ((x - j) & 3) + offset, 16)
            a_ref[pl.ds(start, ref.shape[0]), :] = ref[...]
    for ref, (j, offset) in zip(weights, ((0, 0), (1, 0), (1, 96), (2, 0), (2, 96), (3, 0), (3, 96))):
        start = pl.multiple_of(192 * ((y - j - z) & 3) + offset, 32)
        w_ref[pl.ds(start, ref.shape[0]), :] = ref[...]

    def rows_block(i, carry):
        rows = pl.ds(pl.multiple_of(192 * i, 64), 192)
        lower = pl.ds(pl.multiple_of(192 * i + ROWS, 64), 192)
        values = jnp.concatenate([a_ref[rows, :], a_ref[lower, :]], axis=0)
        acc = lax.dot_general(
            values, w_ref[...], (((1,), (1,)), ((), ())), preferred_element_type=F32
        )
        for n in range(4):
            block = acc[:, 192 * n : 192 * (n + 1)]
            packed = jnp.concatenate([block[0:192], block[192:ROWS]], axis=1)
            outs[n][rows, :] = packed.astype(outs[n].dtype)
        return carry

    lax.fori_loop(0, 2, rows_block, 0)


def place_body(s_ref, r0, r1, r2, r3, slots_ref, text_ref, tslots_ref, own_ref, sib_ref, rows_ref, both_ref):
    y, x, c = s_ref[0], s_ref[1], s_ref[2]

    def positions(core):
        row = lax.broadcasted_iota(jnp.int32, (448, 1), 0)
        k = (row >= 112).astype(jnp.int32) + (row >= 224).astype(jnp.int32) + (row >= 336).astype(jnp.int32)
        return 112 * (8 * y + 2 * ((x + k) & 3) + core) + row - 112 * k

    def pick(position, slots):
        return jnp.where(position == slots, 1.0, 0.0).astype(BF)

    for k, r in enumerate((r0, r1, r2, r3)):
        start = pl.multiple_of(ROWS * ((y - k) & 3), ROWS)
        both = r[...]
        rows_ref[pl.ds(start, r.shape[0]), :] = both[:, 0:192]
        rows_ref[pl.ds(4 * ROWS + start, r.shape[0]), :] = both[:, 192:384]

    def core_block(n, carry):
        where = positions(jnp.where(n == 0, c, 1 - c))
        value = cdot(pick(where, slots_ref[...]), rows_ref[...])
        value = value + cdot(pick(where, tslots_ref[...]), text_ref[...])
        both_ref[n] = value.astype(BF)
        return carry

    lax.fori_loop(0, 2, core_block, 0)
    own_ref[...] = both_ref[0]
    sib_ref[...] = both_ref[1]


def stream_body(s_ref, b0, b1, b2, b3, out_ref, squares_ref):
    x, c = s_ref[1], s_ref[2]
    width = b0.shape[1]
    total = jnp.zeros((b0.shape[0], 1), F32)
    blocks = [b0[...], b1[...], b2[...], b3[...]]
    for place in range(4):
        k = (x - place) & 3
        value = blocks[0]
        for n in range(1, 4):
            value = jnp.where(k == n, blocks[n], value)
        turned = jnp.concatenate([value[:, 192:384], value[:, 0:192]], axis=1)
        value = jnp.where(c == 0, value, turned)
        out_ref[:, width * place : width * (place + 1)] = value
        wide = value.astype(F32)
        total = total + jnp.sum(wide * wide, axis=1, keepdims=True)
    squares_ref[...] = jnp.broadcast_to(total, squares_ref.shape)


def after(values):
    return lax.optimization_barrier(values)


def over_z(value):
    return [value] + [shift(value, "z", k) for k in (1, 2, 3)]


def ring(value, axis):
    half = value.shape[0] // 2
    back = shift(value, axis, 1)
    ahead = shift(value, axis, 3)
    return [value, back, shift(back[:half], axis, 1), shift(ahead[half:], axis, 3), ahead]


def per_device(
    patches,
    norm_gain,
    query_weight,
    key_weight,
    value_weight,
    out_weight,
    layer_scale,
    merge_gain,
    merge_bias,
    proj_weight,
    proj_bias,
    text_rows,
    stream_gain,
    tile_counts,
    image_slots,
    text_slots,
):
    y, x, c, z = [lax.axis_index(name).astype(jnp.int32) for name in ("y", "x", "c", "z")]
    coords = jnp.stack([y, x, c, z])
    width = patches.shape[1]
    share = width // 4

    kvq = project_qkv(coords, patches, norm_gain.reshape(width // HD, HD), key_weight, value_weight, query_weight)

    kvq, out_weight = after((kvq, out_weight))
    moved = [kvq[0]] + [shift(kvq[k], "y", k) for k in (1, 2, 3)]
    windows = call(
        window_body,
        jax.ShapeDtypeStruct((4, out_weight.shape[0] // 2, WINDOW), BF),
        0.1,
        in_specs=[SMEM, VMEM],
    )(coords, out_weight)
    windows, *moved = after((windows, *moved))
    kv_own, q_own = call(
        pack_body,
        (
            jax.ShapeDtypeStruct((4, ROWS, 2 * HD), BF),
            jax.ShapeDtypeStruct((4, ROWS, HD), BF),
        ),
        1,
        in_specs=[VMEM] * 4,
    )(*moved)
    kv_own, q_own, proj_turned = after((kv_own, q_own, proj_weight.T))
    proj_low, proj_high = proj_turned[0:96], proj_turned[96:192]
    back_low, ahead_high = shift(proj_low, "y", 1), shift(proj_high, "y", 3)
    near = [shift(kv_own, "x", 1), shift(kv_own, "x", 3)]
    kv_sib = swap(kv_own)

    where = (coords, tile_counts, q_own)
    state = attend((0,) * 4, *where, [kv_own, kv_sib], None, False)
    near, state, windows, back_low, ahead_high, proj_low, proj_high, kv_here = after(
        (near, state, windows, back_low, ahead_high, proj_low, proj_high, kv_own)
    )
    back_high, ahead_low = shift(proj_high, "y", 1), shift(proj_low, "y", 3)
    out_half = lax.all_to_all(windows, "z", 0, 0, tiled=True)
    far = shift(kv_here, "x", 2)
    blocks = [near[0], swap(near[0]), near[1], swap(near[1])]
    state = attend((1,) * 4 + (3,) * 4, *where, blocks, state, False)
    far, state, out_half, back_low, ahead_high, back_high, ahead_low = after(
        (far, state, out_half, back_low, ahead_high, back_high, ahead_low)
    )
    proj_parts = [
        proj_turned,
        back_low,
        back_high,
        shift(back_low, "y", 1),
        shift(ahead_high, "y", 3),
        ahead_low,
        ahead_high,
    ]
    swap_half = swap(out_half)
    attended = attend((2,) * 4, *where, [far, swap(far)], state, True)
    attended, proj_parts, swap_half = after((attended, proj_parts, swap_half))
    heads = jnp.stack([attended[0]] + [shift(attended[k], "y", 4 - k) for k in (1, 2, 3)])
    heads, merge_gain, merge_bias, layer_scale = after((heads, merge_gain, merge_bias, layer_scale))

    head_parts = [heads] + [shift(heads, "z", k) for k in (1, 2, 3)]
    affine = call(
        turn_body, jax.ShapeDtypeStruct((8, share), F32), 1, in_specs=[VMEM] * 2
    )(merge_gain.reshape(share, 4), merge_bias.reshape(share, 4))
    *head_parts, affine = after((*head_parts, affine))
    residual, stats = call(
        out_body,
        (
            jax.ShapeDtypeStruct((4, MROWS, share), F32),
            jax.ShapeDtypeStruct((MROWS, HD), F32),
        ),
        6,
        scratch=[
            pltpu.VMEM((4, 4 * HD, WINDOW), BF),
            pltpu.VMEM((ROWS, WINDOW), BF),
            pltpu.SemaphoreType.DMA((3,)),
        ],
        in_specs=[SMEM] + [VMEM] * 4 + [ANY] * 3 + [VMEM],
    )(coords, *head_parts, out_half, swap_half, patches, layer_scale[None])
    merged = call(
        merge_body, jax.ShapeDtypeStruct((MROWS, width), BF), 1, in_specs=[VMEM] * 6
    )(*over_z(stats), residual, affine)

    merged_parts = ring(merged, "x")
    merged, image_slots, text_rows, proj_bias = after((merged, image_slots, text_rows, proj_bias))
    turn = [(4 * a + b, 4 * b + a) for a in range(4) for b in range(4)]
    text = lax.ppermute(text_rows, ("y", "z"), turn)
    bias_row = lax.ppermute(proj_bias[None], ("y", "z"), turn)
    slots = image_slots.reshape(16, 2, MROWS).transpose(1, 0, 2).reshape(1, 32 * MROWS)
    bias_row = jnp.concatenate([bias_row, bias_row], axis=1)
    merged_parts += [swap(part) for part in merged_parts]
    *merged_parts, slots, text, bias_row = after((*merged_parts, slots, text, bias_row))
    summed, *partial = call(
        projection_body,
        [jax.ShapeDtypeStruct((ROWS, ROWS), kind) for kind in (F32, BF, BF, BF)],
        8,
        scratch=[pltpu.VMEM((2 * ROWS, width), BF), pltpu.VMEM((2 * ROWS, width), BF)],
        in_specs=[SMEM] + [VMEM] * 17,
    )(coords, *merged_parts, *proj_parts)
    for k in (1, 2, 3):
        summed = summed + shift(partial[k - 1], "z", k).astype(F32)

    rows = jax.nn.gelu(summed + bias_row, approximate=False).astype(BF)

    row_parts = [rows] + [shift(rows, "y", k) for k in (1, 2, 3)]
    placed, for_sibling = call(
        place_body,
        (
            jax.ShapeDtypeStruct((448, 192), BF),
            jax.ShapeDtypeStruct((448, 192), BF),
        ),
        4,
        scratch=[pltpu.VMEM((8 * ROWS, 192), BF), pltpu.VMEM((2, 448, 192), BF)],
        in_specs=[SMEM] + [VMEM] * 7,
    )(coords, *row_parts, slots, text, text_slots[None])
    placed = jnp.concatenate([placed, swap(for_sibling)], axis=1).reshape(4, 112, ROWS)
    blocks = [placed[0]] + [shift(placed[k], "x", k) for k in (1, 2, 3)]
    stream, squares = call(
        stream_body,
        (
            jax.ShapeDtypeStruct((112, 4 * ROWS), BF),
            jax.ShapeDtypeStruct((112, HD), F32),
        ),
        2,
        in_specs=[SMEM] + [VMEM] * 4,
    )(coords, *blocks)
    squares = over_z(squares)
    squares = ((squares[0] + squares[2]) + (squares[1] + squares[3]))[:, 0:1]
    inverse_rms = lax.rsqrt(squares * (1.0 / 6144) + 1e-05)
    normed = (stream.astype(F32) * inverse_rms * stream_gain).astype(BF)
    return (stream, normed)


def solution(mesh):
    grid = Mesh(mesh.devices.reshape(4, 4, 2, 4), ("y", "x", "c", "z"))
    seq = ("y", "x", "c")
    return jax.shard_map(
        per_device,
        mesh=grid,
        in_specs=(
            P(seq, None),
            P(),
            P(None, "z"),
            P(None, "z"),
            P(None, "z"),
            P("z", None),
            P(),
            P("z"),
            P("z"),
            P("z", seq),
            P(seq),
            P(None, seq),
            P("z"),
            P(),
            P(),
            P(),
        ),
        out_specs=(P(seq, "z"), P(seq, "z")),
        check_vma=False,
    )
```

```python
import jax
import jax.numpy as jnp
from jax import lax
from jax.experimental import pallas as pl
from jax.experimental.pallas import tpu as pltpu
from jax.sharding import Mesh, PartitionSpec as P

HD = 128
ROWS = 384
MROWS = 96
BF = jnp.bfloat16
F32 = jnp.float32
LIMIT = 60 * 1024 * 1024


def cdot(a, b):
    return jnp.dot(a, b, preferred_element_type=F32)


def shift(value, axis, k):
    return lax.ppermute(value, axis, [(i, (i + k) % 4) for i in range(4)])


def swap(value):
    return lax.ppermute(value, "c", [(0, 1), (1, 0)])


def cost(us):
    return pl.CostEstimate(flops=int(us * 1.0e9), transcendentals=0, bytes_accessed=0)


def call(body, out_shape, us, scratch=(), **kw):
    return pl.pallas_call(
        body,
        out_shape=out_shape,
        scratch_shapes=scratch,
        cost_estimate=cost(us),
        compiler_params=pltpu.CompilerParams(vmem_limit_bytes=LIMIT),
        **kw,
    )


SMEM = pl.BlockSpec(memory_space=pltpu.SMEM)
VMEM = pl.BlockSpec(memory_space=pltpu.VMEM)
ANY = pl.BlockSpec(memory_space=pl.ANY)


def sub_row_permutation():
    row = lax.broadcasted_iota(jnp.int32, (ROWS, ROWS), 0)
    col = lax.broadcasted_iota(jnp.int32, (ROWS, ROWS), 1)
    sub = (row >= 96).astype(jnp.int32) + (row >= 192).astype(jnp.int32) + (row >= 288).astype(jnp.int32)
    m = row - 96 * sub
    source = (2 * (m >> 4) + (sub >> 1)) * 32 + 2 * (m & 15) + (sub & 1)
    return jnp.where(source == col, 1.0, 0.0).astype(BF)


def qkv_body(s_ref, x_ref, g_ref, wk_ref, wv_ref, wq_ref, o0, o1, o2, o3, xn_ref):
    half = pl.program_id(0)

    @pl.when(half == 0)
    def _():
        xf = cdot(sub_row_permutation(), x_ref[...])
        scale = lax.rsqrt(jnp.mean(xf * xf, axis=-1, keepdims=True) + 1e-06)
        gain = jnp.concatenate([g_ref[i : i + 1] for i in range(g_ref.shape[0])], axis=1)
        xn_ref[...] = (xf * scale * gain).astype(BF)

    xn = xn_ref[...]
    keys = cdot(xn, wk_ref[...]).astype(BF)
    values = cdot(xn, wv_ref[...]).astype(BF)
    queries = (cdot(xn, wq_ref[...]) * HD ** (-0.5)).astype(BF)
    for i in range(2):
        slot = (2 * half + i - s_ref[0]) & 3
        part = slice(HD * i, HD * (i + 1))
        head = jnp.concatenate([keys[:, part], values[:, part], queries[:, part]], axis=1)
        for k, ref in enumerate((o0, o1, o2, o3)):

            @pl.when(slot == k)
            def _(ref=ref, head=head):
                ref[...] = head


def project_qkv(y, patches, gain, wk, wv, wq):
    width = patches.shape[1]
    whole = pl.BlockSpec((ROWS, width), lambda j, s: (0, 0))
    weight = pl.BlockSpec((width, 2 * HD), lambda j, s: (0, j))
    return pl.pallas_call(
        qkv_body,
        out_shape=[jax.ShapeDtypeStruct((ROWS, 3 * HD), BF)] * 4,
        grid_spec=pltpu.PrefetchScalarGridSpec(
            num_scalar_prefetch=1,
            grid=(2,),
            in_specs=[whole, pl.BlockSpec((width // HD, HD), lambda j, s: (0, 0)), weight, weight, weight],
            out_specs=[pl.BlockSpec((ROWS, 3 * HD), lambda j, s: (0, 0))] * 4,
            scratch_shapes=[pltpu.VMEM((ROWS, width), BF)],
        ),
        cost_estimate=cost(11),
        compiler_params=pltpu.CompilerParams(
            dimension_semantics=("arbitrary",), vmem_limit_bytes=LIMIT
        ),
    )(y, patches, gain, wk, wv, wq)


def image_lanes(info, scale, same):
    row = lax.broadcasted_iota(jnp.int32, (ROWS, HD), 0)
    lane = lax.broadcasted_iota(jnp.int32, (ROWS, HD), 1)
    sub = (row >= 96).astype(jnp.int32) + (row >= 192).astype(jnp.int32) + (row >= 288).astype(jnp.int32)
    image = jnp.where((row - 96 * sub) * 4 < info[2], info[0], info[1])
    hit = lane == image if same else lane != image
    return jnp.where(hit, scale, 0.0).astype(BF)


def attention_body(steps, first, last, s_ref, t_ref, q_ref, *refs):
    rest = refs[:-3]
    own_ref, sib_ref, list_ref = refs[-3:]
    filled = 0
    while filled < len(steps):
        own, sib = rest[:2]
        rest = rest[2:]
        own_ref[filled : filled + own.shape[0]] = own[...]
        sib_ref[filled : filled + own.shape[0]] = sib[...]
        filled += own.shape[0]
    if not first:
        acc_in, max_in = rest[:2]
        rest = rest[2:]
    if last:
        *o_refs, acc_ref, max_ref = rest
    else:
        acc_ref, max_ref = rest
    if first:
        acc_ref[...] = jnp.zeros(acc_ref.shape, F32)
        max_ref[...] = jnp.full(max_ref.shape, -1e30, F32)
    else:
        acc_ref[...] = acc_in[...]
        max_ref[...] = max_in[...]
    y, x, c = s_ref[0], s_ref[1], s_ref[2]
    bound0 = 1024 * t_ref[0]
    bound1 = 1024 * (t_ref[0] + t_ref[1])

    def image_of(row):
        return (row >= bound0).astype(jnp.int32) + (row >= bound1).astype(jnp.int32)

    def block(yy, xx, cc):
        base = ROWS * (8 * yy + 2 * xx + cc)
        return image_of(base), image_of(base + ROWS - 1), 1024 - (base & 1023)

    def blocks_of(i):
        qb = i & 3
        kr = i >> 2
        step = steps[0] if len(steps) == 4 else jnp.where(kr < 4, steps[0], steps[4])
        xk = (x - step) & 3
        ki = [block((y - kr) & 3, xk, cc) for cc in (c, 1 - c)]
        return qb, kr, block((y - qb) & 3, x, c), ki

    def note(i, count):
        qb, kr, qi, ki = blocks_of(i)
        low = jnp.minimum(ki[0][0], ki[1][0])
        high = jnp.maximum(ki[0][1], ki[1][1])
        meets = jnp.logical_and(qi[1] >= low, qi[0] <= high)
        list_ref[count] = i
        return count + meets.astype(jnp.int32)

    def score(i, live):
        qb, kr, qi, ki = blocks_of(i)
        qi = (jnp.where(live, qi[0], 99), jnp.where(live, qi[1], 99), qi[2])
        q = jnp.concatenate([q_ref[qb], image_lanes(qi, -1e30, False)], axis=1)
        keys, values = [], []
        for n, ref in enumerate((own_ref, sib_ref)):
            keys.append(jnp.concatenate([ref[kr, :, 0:HD], image_lanes(ki[n], 1.0, True)], axis=1))
            values.append(
                jnp.concatenate([ref[kr, :, HD : 2 * HD], jnp.ones((ROWS, HD), BF)], axis=1)
            )
        scores = lax.dot_general(
            q, jnp.concatenate(keys, axis=0), (((1,), (1,)), ((), ())), preferred_element_type=F32
        )
        return qb, scores, jnp.concatenate(values, axis=0)

    def fold(qb, scores, values):
        old = max_ref[qb]
        new = jnp.maximum(old, jnp.max(scores, axis=1, keepdims=True))
        factor = jnp.exp(old - new)
        weights = jnp.exp(scores - new[:, 0:1]).astype(BF)
        max_ref[qb] = new
        acc_ref[qb] = acc_ref[qb] * jnp.concatenate([factor, factor], axis=1) + cdot(weights, values)

    def alone(t, carry):
        fold(*score(list_ref[t], True))
        return carry

    def two(t, carry):
        odd = 2 * t + 1 < count
        one = score(list_ref[2 * t], True)
        other = score(list_ref[jnp.where(odd, 2 * t + 1, 2 * t)], odd)
        fold(*one)
        fold(*other)
        return carry

    count = lax.fori_loop(0, 4 * len(steps), note, jnp.int32(0))
    if first:
        lax.fori_loop(0, count, alone, 0)
    else:
        lax.fori_loop(0, (count + 1) >> 1, two, 0)
    if last:
        for b in range(4):
            o_refs[b][...] = (acc_ref[b, :, 0:HD] / acc_ref[b, :, HD : 2 * HD]).astype(BF)


def attend(steps, coords, tile_counts, q, blocks, state, last):
    first = state is None
    state_shapes = [
        jax.ShapeDtypeStruct((4, ROWS, 2 * HD), F32),
        jax.ShapeDtypeStruct((4, ROWS, HD), F32),
    ]
    args = [coords, tile_counts, q, *blocks] + ([] if first else list(state))

    def body(*refs):
        attention_body(steps, first, last, *refs)

    specs = [SMEM, SMEM] + [VMEM] * (len(args) - 2)
    held = [pltpu.VMEM((len(steps), ROWS, 2 * HD), BF)] * 2 + [pltpu.SMEM((64,), jnp.int32)]
    if last:
        return call(
            body,
            [jax.ShapeDtypeStruct((ROWS, HD), BF)] * 4,
            (4 if len(steps) == 8 else 2.5 * len(steps)),
            scratch=[pltpu.VMEM(s.shape, s.dtype) for s in state_shapes] + held,
            in_specs=specs,
        )(*args)
    return call(body, state_shapes, (4 if len(steps) == 8 else 2.5 * len(steps)), scratch=held, in_specs=specs)(*args)


def pack_body(m0, m1, m2, m3, kv_ref, q_ref):
    for k, ref in enumerate((m0, m1, m2, m3)):
        kv_ref[k] = ref[:, 0 : 2 * HD]
        q_ref[k] = ref[:, 2 * HD : 3 * HD]


def turn_body(gain_ref, bias_ref, out_ref):
    out_ref[0:4] = gain_ref[...].T
    out_ref[4:8] = bias_ref[...].T


WINDOW = 896


def window(z):
    return pl.ds(pl.multiple_of(768 * z, HD), WINDOW)


def window_body(s_ref, w_ref, out_ref):
    half = out_ref.shape[1]
    rows = pl.ds(pl.multiple_of(half * s_ref[2], 64), half)
    for i in range(4):
        out_ref[i] = w_ref[rows, 768 * i : 768 * i + WINDOW]


def out_body(s_ref, o0, o1, o2, o3, mine, other, x_any, scale_ref, r_ref, stats_ref, w_ref, x_ref, sems):
    y, c, z = s_ref[0], s_ref[2], s_ref[3]
    half = mine.shape[1]
    upper = pl.ds(pl.multiple_of(half * c, 64), half)
    lower = pl.ds(pl.multiple_of(half * (1 - c), 64), half)
    copies = [
        pltpu.make_async_copy(mine, w_ref.at[:, upper], sems.at[0]),
        pltpu.make_async_copy(other, w_ref.at[:, lower], sems.at[1]),
        pltpu.make_async_copy(x_any.at[:, window(z)], x_ref, sems.at[2]),
    ]
    for copy in copies:
        copy.start()
    acc = jnp.zeros((ROWS, WINDOW), F32)
    for copy in copies:
        copy.wait()
    parts = [
        [o0[k] for k in range(4)],
        [o1[k] for k in range(4)],
        [o2[k] for k in range(4)],
        [o3[k] for k in range(4)],
    ]
    for j in range(4):
        heads = jnp.concatenate(parts[j], axis=1)
        plane = (z - j) & 3
        rows = jnp.concatenate(
            [w_ref[plane, pl.ds(pl.multiple_of(HD * ((y + k) & 3), HD), HD), :] for k in range(4)],
            axis=0,
        )
        acc = acc + cdot(heads, rows)
    residual = cdot(sub_row_permutation(), x_ref[...]) + scale_ref[:, window(z)] * acc
    residual = pltpu.roll(residual, WINDOW - 32 * z, 1)[:, 0 : r_ref.shape[2]]
    total = jnp.zeros((MROWS, 1), F32)
    squares = jnp.zeros((MROWS, 1), F32)
    for sub in range(4):
        part = residual[MROWS * sub : MROWS * (sub + 1)]
        r_ref[sub] = part
        total = total + jnp.sum(part, axis=1, keepdims=True)
        squares = squares + jnp.sum(part * part, axis=1, keepdims=True)
    lane = lax.broadcasted_iota(jnp.int32, (MROWS, HD), 1)
    stats_ref[...] = jnp.where(lane == 0, total, squares)


def interleave(parts):
    count = parts[0].shape[1]
    row = lax.broadcasted_iota(jnp.int32, (4 * count, 4 * count), 0)
    col = lax.broadcasted_iota(jnp.int32, (4 * count, 4 * count), 1)
    hit = row == (col & 3) * count + (col >> 2)
    return cdot(jnp.concatenate(parts, axis=1), jnp.where(hit, 1.0, 0.0).astype(BF)).astype(BF)


def merge_body(s0, s1, s2, s3, r_ref, affine_ref, out_ref):
    share = r_ref.shape[2]
    stats = ((s0[...] + s2[...]) + (s1[...] + s3[...])) * (1.0 / (16 * share))
    mean = stats[:, 0:1]
    scale = lax.rsqrt(stats[:, 1:2] - mean * mean + 1e-05)
    normed = []
    for sub in range(4):
        gain, bias = affine_ref[sub : sub + 1], affine_ref[4 + sub : 5 + sub]
        normed.append(((r_ref[sub] - mean) * scale * gain + bias).astype(BF))
    for start in range(0, share, HD):
        stop = min(start + HD, share)
        out_ref[:, 4 * start : 4 * stop] = interleave([n[:, start:stop] for n in normed])


def projection_body(s_ref, *refs):
    merged = refs[:10]
    weights = refs[10:17]
    outs = refs[17:21]
    a_ref, w_ref = refs[21:]
    y, x, c, z = s_ref[0], s_ref[1], s_ref[2], s_ref[3]
    for n, core in ((0, c), (5, 1 - c)):
        for part, (j, offset) in enumerate(((0, 0), (1, 0), (2, 0), (2, 48), (3, 0))):
            ref = merged[n + part]
            start = pl.multiple_of(ROWS * core + MROWS * ((x - j) & 3) + offset, 16)
            a_ref[pl.ds(start, ref.shape[0]), :] = ref[...]
    for ref, (j, offset) in zip(weights, ((0, 0), (1, 0), (1, 96), (2, 0), (2, 96), (3, 0), (3, 96))):
        start = pl.multiple_of(192 * ((y - j - z) & 3) + offset, 32)
        w_ref[pl.ds(start, ref.shape[0]), :] = ref[...]

    def rows_block(i, carry):
        rows = pl.ds(pl.multiple_of(192 * i, 64), 192)
        lower = pl.ds(pl.multiple_of(192 * i + ROWS, 64), 192)
        values = jnp.concatenate([a_ref[rows, :], a_ref[lower, :]], axis=0)
        acc = lax.dot_general(
            values, w_ref[...], (((1,), (1,)), ((), ())), preferred_element_type=F32
        )
        for n in range(4):
            block = acc[:, 192 * n : 192 * (n + 1)]
            packed = jnp.concatenate([block[0:192], block[192:ROWS]], axis=1)
            outs[n][rows, :] = packed.astype(outs[n].dtype)
        return carry

    lax.fori_loop(0, 2, rows_block, 0)


def place_body(s_ref, r0, r1, r2, r3, slots_ref, text_ref, tslots_ref, own_ref, sib_ref, rows_ref, both_ref):
    y, x, c = s_ref[0], s_ref[1], s_ref[2]

    def positions(core):
        row = lax.broadcasted_iota(jnp.int32, (448, 1), 0)
        k = (row >= 112).astype(jnp.int32) + (row >= 224).astype(jnp.int32) + (row >= 336).astype(jnp.int32)
        return 112 * (8 * y + 2 * ((x + k) & 3) + core) + row - 112 * k

    def pick(position, slots):
        return jnp.where(position == slots, 1.0, 0.0).astype(BF)

    for k, r in enumerate((r0, r1, r2, r3)):
        start = pl.multiple_of(ROWS * ((y - k) & 3), ROWS)
        both = r[...]
        rows_ref[pl.ds(start, r.shape[0]), :] = both[:, 0:192]
        rows_ref[pl.ds(4 * ROWS + start, r.shape[0]), :] = both[:, 192:384]

    def core_block(n, carry):
        where = positions(jnp.where(n == 0, c, 1 - c))
        value = cdot(pick(where, slots_ref[...]), rows_ref[...])
        value = value + cdot(pick(where, tslots_ref[...]), text_ref[...])
        both_ref[n] = value.astype(BF)
        return carry

    lax.fori_loop(0, 2, core_block, 0)
    own_ref[...] = both_ref[0]
    sib_ref[...] = both_ref[1]


def stream_body(s_ref, b0, b1, b2, b3, out_ref, squares_ref):
    x, c = s_ref[1], s_ref[2]
    width = b0.shape[1]
    total = jnp.zeros((b0.shape[0], 1), F32)
    blocks = [b0[...], b1[...], b2[...], b3[...]]
    for place in range(4):
        k = (x - place) & 3
        value = blocks[0]
        for n in range(1, 4):
            value = jnp.where(k == n, blocks[n], value)
        turned = jnp.concatenate([value[:, 192:384], value[:, 0:192]], axis=1)
        value = jnp.where(c == 0, value, turned)
        out_ref[:, width * place : width * (place + 1)] = value
        wide = value.astype(F32)
        total = total + jnp.sum(wide * wide, axis=1, keepdims=True)
    squares_ref[...] = jnp.broadcast_to(total, squares_ref.shape)


def after(values):
    return lax.optimization_barrier(values)


def over_z(value):
    return [value] + [shift(value, "z", k) for k in (1, 2, 3)]


def ring(value, axis):
    half = value.shape[0] // 2
    back = shift(value, axis, 1)
    ahead = shift(value, axis, 3)
    return [value, back, shift(back[:half], axis, 1), shift(ahead[half:], axis, 3), ahead]


def per_device(
    patches,
    norm_gain,
    query_weight,
    key_weight,
    value_weight,
    out_weight,
    layer_scale,
    merge_gain,
    merge_bias,
    proj_weight,
    proj_bias,
    text_rows,
    stream_gain,
    tile_counts,
    image_slots,
    text_slots,
):
    y, x, c, z = [lax.axis_index(name).astype(jnp.int32) for name in ("y", "x", "c", "z")]
    coords = jnp.stack([y, x, c, z])
    width = patches.shape[1]
    share = width // 4

    kvq = project_qkv(coords, patches, norm_gain.reshape(width // HD, HD), key_weight, value_weight, query_weight)

    kvq, out_weight = after((kvq, out_weight))
    moved = [kvq[0]] + [shift(kvq[k], "y", k) for k in (1, 2, 3)]
    windows = call(
        window_body,
        jax.ShapeDtypeStruct((4, out_weight.shape[0] // 2, WINDOW), BF),
        0.1,
        in_specs=[SMEM, VMEM],
    )(coords, out_weight)
    windows, *moved = after((windows, *moved))
    kv_own, q_own = call(
        pack_body,
        (
            jax.ShapeDtypeStruct((4, ROWS, 2 * HD), BF),
            jax.ShapeDtypeStruct((4, ROWS, HD), BF),
        ),
        1,
        in_specs=[VMEM] * 4,
    )(*moved)
    kv_own, q_own, proj_turned = after((kv_own, q_own, proj_weight.T))
    proj_low, proj_high = proj_turned[0:96], proj_turned[96:192]
    back_low, ahead_high = shift(proj_low, "y", 1), shift(proj_high, "y", 3)
    near = [shift(kv_own, "x", 1), shift(kv_own, "x", 3)]
    kv_sib = swap(kv_own)

    where = (coords, tile_counts, q_own)
    state = attend((0,) * 4, *where, [kv_own, kv_sib], None, False)
    windows, state = after((windows, state))
    out_half = lax.all_to_all(windows, "z", 0, 0, tiled=True)
    near, state, back_low, ahead_high, proj_low, proj_high, kv_here = after(
        (near, state, back_low, ahead_high, proj_low, proj_high, kv_own)
    )
    back_high, ahead_low = shift(proj_high, "y", 1), shift(proj_low, "y", 3)
    far = shift(kv_here, "x", 2)
    blocks = [near[0], swap(near[0]), near[1], swap(near[1])]
    state = attend((1,) * 4 + (3,) * 4, *where, blocks, state, False)
    far, state, out_half, back_low, ahead_high, back_high, ahead_low = after(
        (far, state, out_half, back_low, ahead_high, back_high, ahead_low)
    )
    proj_parts = [
        proj_turned,
        back_low,
        back_high,
        shift(back_low, "y", 1),
        shift(ahead_high, "y", 3),
        ahead_low,
        ahead_high,
    ]
    swap_half = swap(out_half)
    attended = attend((2,) * 4, *where, [far, swap(far)], state, True)
    attended, proj_parts, swap_half = after((attended, proj_parts, swap_half))
    heads = jnp.stack([attended[0]] + [shift(attended[k], "y", 4 - k) for k in (1, 2, 3)])
    heads, merge_gain, merge_bias, layer_scale = after((heads, merge_gain, merge_bias, layer_scale))

    head_parts = [heads] + [shift(heads, "z", k) for k in (1, 2, 3)]
    affine = call(
        turn_body, jax.ShapeDtypeStruct((8, share), F32), 1, in_specs=[VMEM] * 2
    )(merge_gain.reshape(share, 4), merge_bias.reshape(share, 4))
    *head_parts, affine = after((*head_parts, affine))
    residual, stats = call(
        out_body,
        (
            jax.ShapeDtypeStruct((4, MROWS, share), F32),
            jax.ShapeDtypeStruct((MROWS, HD), F32),
        ),
        6,
        scratch=[
            pltpu.VMEM((4, 4 * HD, WINDOW), BF),
            pltpu.VMEM((ROWS, WINDOW), BF),
            pltpu.SemaphoreType.DMA((3,)),
        ],
        in_specs=[SMEM] + [VMEM] * 4 + [ANY] * 3 + [VMEM],
    )(coords, *head_parts, out_half, swap_half, patches, layer_scale[None])
    merged = call(
        merge_body, jax.ShapeDtypeStruct((MROWS, width), BF), 1, in_specs=[VMEM] * 6
    )(*over_z(stats), residual, affine)

    merged_parts = ring(merged, "x")
    merged, image_slots, text_rows, proj_bias = after((merged, image_slots, text_rows, proj_bias))
    turn = [(4 * a + b, 4 * b + a) for a in range(4) for b in range(4)]
    text = lax.ppermute(text_rows, ("y", "z"), turn)
    bias_row = lax.ppermute(proj_bias[None], ("y", "z"), turn)
    slots = image_slots.reshape(16, 2, MROWS).transpose(1, 0, 2).reshape(1, 32 * MROWS)
    bias_row = jnp.concatenate([bias_row, bias_row], axis=1)
    merged_parts += [swap(part) for part in merged_parts]
    *merged_parts, slots, text, bias_row = after((*merged_parts, slots, text, bias_row))
    summed, *partial = call(
        projection_body,
        [jax.ShapeDtypeStruct((ROWS, ROWS), kind) for kind in (F32, BF, BF, BF)],
        8,
        scratch=[pltpu.VMEM((2 * ROWS, width), BF), pltpu.VMEM((2 * ROWS, width), BF)],
        in_specs=[SMEM] + [VMEM] * 17,
    )(coords, *merged_parts, *proj_parts)
    for k in (1, 2, 3):
        summed = summed + shift(partial[k - 1], "z", k).astype(F32)

    rows = jax.nn.gelu(summed + bias_row, approximate=False).astype(BF)

    row_parts = [rows] + [shift(rows, "y", k) for k in (1, 2, 3)]
    placed, for_sibling = call(
        place_body,
        (
            jax.ShapeDtypeStruct((448, 192), BF),
            jax.ShapeDtypeStruct((448, 192), BF),
        ),
        4,
        scratch=[pltpu.VMEM((8 * ROWS, 192), BF), pltpu.VMEM((2, 448, 192), BF)],
        in_specs=[SMEM] + [VMEM] * 7,
    )(coords, *row_parts, slots, text, text_slots[None])
    placed = jnp.concatenate([placed, swap(for_sibling)], axis=1).reshape(4, 112, ROWS)
    blocks = [placed[0]] + [shift(placed[k], "x", k) for k in (1, 2, 3)]
    stream, squares = call(
        stream_body,
        (
            jax.ShapeDtypeStruct((112, 4 * ROWS), BF),
            jax.ShapeDtypeStruct((112, HD), F32),
        ),
        2,
        in_specs=[SMEM] + [VMEM] * 4,
    )(coords, *blocks)
    squares = over_z(squares)
    squares = ((squares[0] + squares[2]) + (squares[1] + squares[3]))[:, 0:1]
    inverse_rms = lax.rsqrt(squares * (1.0 / 6144) + 1e-05)
    normed = (stream.astype(F32) * inverse_rms * stream_gain).astype(BF)
    return (stream, normed)


def solution(mesh):
    grid = Mesh(mesh.devices.reshape(4, 4, 2, 4), ("y", "x", "c", "z"))
    seq = ("y", "x", "c")
    return jax.shard_map(
        per_device,
        mesh=grid,
        in_specs=(
            P(seq, None),
            P(),
            P(None, "z"),
            P(None, "z"),
            P(None, "z"),
            P("z", None),
            P(),
            P("z"),
            P("z"),
            P("z", seq),
            P(seq),
            P(None, seq),
            P("z"),
            P(),
            P(),
            P(),
        ),
        out_specs=(P(seq, "z"), P(seq, "z")),
        check_vma=False,
    )
```
